256 devices in a mesh: gx: 8 (over z), gy: 4 (over x), gz: 8 (over y, core).
Axes of the slice: x: 4, y: 4, z: 8, core: 2. Of those that a mesh axis runs over, the one named last changes fastest.
Arguments:
- rhs_cells: float32 [512, 128, 1024], P('gx', 'gy', 'gz'), may hold values from -4.5 to 4.5
- heat_diag: float32 [512, 128, 1024], P('gx', 'gy', 'gz'), may hold values from 0.5 to 4
- rhs_faces: float32 [4096, 128], P(('gx', 'gy', 'gz')), may hold values from 2 to 8
- emissive: float32 [4096, 128], P(('gx', 'gy', 'gz')), may hold values from 0.5 to 4
- view_factors: float32 [4096, 4, 128, 128], P(('gx', 'gy', 'gz')), may hold values from 0 to 0.00234375
- tile_slots: int32 [4096, 4], P(('gx', 'gy', 'gz')), may hold values from 0 to 127
- read_lists: int32 [256, 32, 4], P(('gx', 'gy', 'gz')), may hold values from 0 to 15
- face_cells: int32 [4096, 128], P(('gx', 'gy', 'gz')), may hold values from 0 to 262143
Outputs:
- sol_cells: float32 [512, 128, 1024], P('gx', 'gy', 'gz')
- sol_faces: float32 [4096, 128], P(('gx', 'gy', 'gz'))
The draws below stay inside these ranges and needn't reach their ends.
Inputs may be any that keep to these rules, and one draw needn't show every extreme that they name: `tile_slots`: entries index the read tiles, owner-major. `read_lists`: local tile numbers on the owner; repeats may occur. `face_cells`: flat cell index within the owning device's block.
All inputs are finite; a program needn't handle non-finite values.
Results may differ from the reference program's by a relative error of at most 0.0003.
Values sent between devices are 32-bit elements; how exact they have to be, the bound alone decides.
No kernel may reach another device: no remote copies, remote signals or barrier semaphores. Data moves between devices by JAX's collectives and lax.ppermute only.
A program may use at most 64 MiB of HBM per device.

```python
import math
import jax
import jax.numpy as jnp
from jax import lax

CX = 64
CY = 32
CZ = 128
FT_DEV = 16
TILE = 128
K_SLOTS = 4
P_READ = 4
ITERS = 3
NX = 512
NY = 128
NZ = 1024
GROUP = 32
NFT = 4096
SLOTS = 128
N_GY = 4
N_GZ = 8
DEVICES = 256


def draw_rhs_cells(key, part):
    ramp = 1.0 + 2.0 * jnp.arange(NX, dtype=jnp.float32) / max(NX - 1, 1)
    base = jnp.clip(jax.random.normal(key, (NX, NY, NZ), jnp.float32), -6.0, 6.0)
    return 0.25 * base * ramp[:, None, None]


def touch_ends(array, key, low, largest):
    spot = [jax.random.randint(jax.random.fold_in(key, axis), (), 0, length) for axis, length in enumerate(array.shape)]
    longest = array.shape.index(max(array.shape))
    beside = spot[:longest] + [(spot[longest] + 1) % array.shape[longest]] + spot[longest + 1:]
    return array.at[tuple(spot)].set(low).at[tuple(beside)].set(largest)


def block_scale(rng, shape, shards, low, largest):
    factor_of, own = 1.0, jax.random.fold_in(rng, 6)
    for position, parts in shards:
        draws = jnp.exp(jax.random.uniform(jax.random.fold_in(own, position), (parts,), jnp.float32, low / len(shards), largest / len(shards)))
        factor_of = factor_of * jnp.repeat(draws, shape[position] // parts).reshape([-1 if axis == position else 1 for axis in range(len(shape))])
    return factor_of


def setup_inputs(seed: int = 0) -> dict:
    key_of = jax.random.split(jax.random.key(seed), 9)
    return {
        "rhs_cells": draw_rhs_cells(jax.random.fold_in(key_of[8], 71), 0),
        "heat_diag": jnp.clip(jnp.exp(math.log(4.0) - 2.0794415 * jax.random.uniform(key_of[1], (NX, NY, NZ), jnp.float32) ** block_scale(key_of[1], (NX, NY, NZ), ((0, 8), (1, 4), (2, 8)), -0.2, 0.2)), 0.5, 4.0),
        "rhs_faces": jnp.clip(2.0 + 6.0 * jax.random.uniform(key_of[2], (NFT, TILE), jnp.float32) ** block_scale(key_of[2], (NFT, TILE), ((0, 256),), -0.2, 0.2), 2.0, 8.0),
        "emissive": jnp.clip(jnp.exp(math.log(4.0) - 2.0794415 * jax.random.uniform(key_of[3], (NFT, TILE), jnp.float32) ** block_scale(key_of[3], (NFT, TILE), ((0, 256),), -0.2, 0.2)), 0.5, 4.0),
        "view_factors": jnp.clip(0.00234375 * jax.random.uniform(key_of[4], (NFT, K_SLOTS, TILE, TILE), jnp.float32) ** block_scale(key_of[4], (NFT, K_SLOTS, TILE, TILE), ((0, 256),), -0.2, 0.2), 0.0, 0.00234375),
        "tile_slots": touch_ends(jax.random.randint(key_of[5], (NFT, K_SLOTS), 0, SLOTS), jax.random.fold_in(key_of[5], 1), 0, SLOTS - 1).astype(jnp.int32),
        "read_lists": touch_ends(jax.random.randint(key_of[6], (DEVICES, GROUP, P_READ), 0, FT_DEV), jax.random.fold_in(key_of[6], 1), 0, FT_DEV - 1).astype(jnp.int32),
        "face_cells": touch_ends(jax.random.randint(key_of[7], (NFT, TILE), 0, CX * CY * CZ), jax.random.fold_in(key_of[7], 1), 0, (CX * CY * CZ) - 1).astype(jnp.int32),
    }


def least_squares(hess, beta):
    gram = [[sum((hess[r][a] * hess[r][b] for r in range(ITERS + 1))) for b in range(ITERS)] for a in range(ITERS)]
    target = [beta * hess[0][a] for a in range(ITERS)]
    for col in range(ITERS):
        for row in range(col + 1, ITERS):
            factor = gram[row][col] / gram[col][col]
            gram[row] = [gram[row][b] - factor * gram[col][b] for b in range(ITERS)]
            target[row] = target[row] - factor * target[col]
    coeffs = [None] * ITERS
    for row in range(ITERS - 1, -1, -1):
        acc = target[row]
        for b in range(row + 1, ITERS):
            acc = acc - gram[row][b] * coeffs[b]
        coeffs[row] = acc / gram[row][row]
    return coeffs

def reference(rhs_cells, heat_diag, rhs_faces, emissive, view_factors, tile_slots, read_lists, face_cells):
    tiles = jnp.arange(NFT, dtype=jnp.int32)
    device = (tiles // FT_DEV).astype(jnp.int32)
    slab = device // GROUP
    owner = tile_slots // P_READ
    within = tile_slots % P_READ
    column = (slab[:, None] * GROUP + owner) * FT_DEV + read_lists[device[:, None], owner, within]
    dev_x = (device // (N_GY * N_GZ))[:, None]
    dev_y = (device // N_GZ % N_GY)[:, None]
    dev_z = (device % N_GZ)[:, None]
    cell_x = dev_x * CX + face_cells // (CY * CZ)
    cell_y = dev_y * CY + face_cells // CZ % CY
    cell_z = dev_z * CZ + face_cells % CZ

    def operate(pair):
        field, faces = pair
        padded = jnp.pad(field, 1)
        beside = padded[2:, 1:-1, 1:-1] + padded[:-2, 1:-1, 1:-1]
        beside = beside + padded[1:-1, 2:, 1:-1] + padded[1:-1, :-2, 1:-1]
        beside = beside + padded[1:-1, 1:-1, 2:] + padded[1:-1, 1:-1, :-2]
        under = field[cell_x, cell_y, cell_z]
        cells = ((6.0 + heat_diag) * field - beside).at[cell_x, cell_y, cell_z].add(1.0 * (under - faces))
        seen = faces[column]
        flux = jnp.einsum('ikab,ikb->ia', view_factors, seen, precision=lax.Precision.HIGHEST)
        out_faces = (1.0 + emissive) * faces - under - emissive * flux
        return (cells, out_faces)

    def inner(a, b):
        return jnp.sum(a[0] * b[0]) + jnp.sum(a[1] * b[1])
    start = (rhs_cells, rhs_faces)
    beta = jnp.sqrt(inner(start, start))
    basis = [(rhs_cells / beta, rhs_faces / beta)]
    hess = [[jnp.float32(0.0) for j in range(ITERS)] for i in range(ITERS + 1)]
    for j in range(ITERS):
        work = operate(basis[j])
        dots = [inner(basis[i], work) for i in range(j + 1)]
        for i in range(j + 1):
            hess[i][j] = dots[i]
            work = (work[0] - dots[i] * basis[i][0], work[1] - dots[i] * basis[i][1])
        length = jnp.sqrt(inner(work, work))
        hess[j + 1][j] = length
        if j + 1 < ITERS:
            basis.append((work[0] / length, work[1] / length))
    coeffs = least_squares(hess, beta)
    sol_cells = sum((coeffs[j] * basis[j][0] for j in range(ITERS)))
    sol_faces = sum((coeffs[j] * basis[j][1] for j in range(ITERS)))
    return (sol_cells, sol_faces)
```

```python
import functools

import jax
import jax.numpy as jnp
from jax import lax
from jax.experimental import pallas as pl
from jax.experimental.pallas import tpu as pltpu
from jax.sharding import PartitionSpec as P

ITERS = 3
SHIFTS = (6.0, 3.0, 11.0)
SCALE = 0.125
CX, CY, CZ = 64, 32, 128
ROWS = CX * CY
TILES = 16
TILE = 128
FACES = TILES * TILE
SLOTS = 4
PER_OWNER = 4
f32 = jnp.float32
bf16 = jnp.bfloat16
VMEM = pl.BlockSpec(memory_space=pltpu.VMEM)
SMEM = pl.BlockSpec(memory_space=pltpu.SMEM)


def params(mib):
    return pltpu.CompilerParams(vmem_limit_bytes=mib << 20)


def split(x):
    high = x.astype(bf16)
    return high, (x - high.astype(f32)).astype(bf16)


def iota(shape, dim):
    return lax.broadcasted_iota(jnp.int32, shape, dim)


def pack_edges(block, x, lane, low_y, high_y, low_z, high_z):
    low_y[pl.ds(x, 1), :] = block[0:1, :]
    high_y[pl.ds(x, 1), :] = block[CY - 1 : CY, :]
    here = lane == x
    low_z[...] = jnp.where(here, pltpu.roll(block, x, 1), low_z[...])
    high_z[...] = jnp.where(here, pltpu.roll(block, x + 1, 1), high_z[...])


def edges_body(u, low_y, high_y, low_z, high_z):
    low_z[...] = jnp.zeros((CY, CZ), f32)
    high_z[...] = jnp.zeros((CY, CZ), f32)
    lane = iota((CY, CZ), 1)

    def plane(x, carry):
        pack_edges(u[x], x, lane, low_y, high_y, low_z, high_z)
        return carry

    lax.fori_loop(0, CX, plane, 0, unroll=4)


EDGE_SHAPES = (
    jax.ShapeDtypeStruct((CX, CZ), f32),
    jax.ShapeDtypeStruct((CX, CZ), f32),
    jax.ShapeDtypeStruct((CY, CZ), f32),
    jax.ShapeDtypeStruct((CY, CZ), f32),
)


def edges(u):
    return pl.pallas_call(
        edges_body, out_shape=EDGE_SHAPES, in_specs=[VMEM], out_specs=(VMEM,) * 4, name="edges"
    )(u)


def meet(u, s, rows, place, count, spread, under, wide):
    z = iota((CZ, TILE), 0)
    for i in range(TILES):
        at = pl.ds(i * TILE, TILE)
        here = z == (place[i : i + 1, :] & (CZ - 1))
        high, low = split(s[i : i + 1, :])
        spread[0:CZ, at] = jnp.where(here, high.astype(f32), 0.0).astype(bf16)
        spread[CZ : 2 * CZ, at] = jnp.where(here, low.astype(f32), 0.0).astype(bf16)
        if count:
            spread[2 * CZ : 3 * CZ, at] = jnp.where(here, 1.0, 0.0).astype(bf16)
        part = u[pl.ds(i * TILE, TILE), :].T
        high, low = split(part)
        wide[0:CZ, at] = high
        wide[CZ : 2 * CZ, at] = low
    seen = jnp.dot(wide[...], rows[...], preferred_element_type=f32)
    for i in range(TILES):
        here = z == (place[i : i + 1, :] & (CZ - 1))
        at = slice(i * TILE, (i + 1) * TILE)
        both = seen[0:CZ, at] + seen[CZ : 2 * CZ, at]
        under[i : i + 1, :] = jnp.sum(jnp.where(here, both, 0.0), axis=0, keepdims=True)
    return lax.dot_general(
        rows[...], spread[...], (((1,), (1,)), ((), ())), preferred_element_type=f32
    )


def first_body(u, s, place, heat, rows, diag, base, under, spread, wide):
    number = iota((ROWS, TILE), 0)
    for i in range(TILES):
        row = lax.shift_right_logical(place[i : i + 1, :], 7)
        rows[:, pl.ds(i * TILE, TILE)] = jnp.where(number == row, 1.0, 0.0).astype(bf16)
    sums = meet(u, s, rows, place, True, spread, under, wide)
    total = 6.0 + heat[...] + sums[:, 2 * CZ : 3 * CZ]
    diag[...] = total
    base[...] = (total - SHIFTS[0]) * u[...] - (sums[:, 0:CZ] + sums[:, CZ : 2 * CZ])


def later_body(shift, u, s, place, diag, rows, base, under, spread, wide):
    sums = meet(u, s, rows, place, False, spread, under, wide)
    base[...] = (diag[...] - shift) * u[...] - (sums[:, 0:CZ] + sums[:, CZ : 2 * CZ])


def scratch(blocks):
    return [pltpu.VMEM((blocks * CZ, FACES), bf16), pltpu.VMEM((2 * CZ, FACES), bf16)]


FIELD = jax.ShapeDtypeStruct((ROWS, CZ), f32)
ON_FACES = jax.ShapeDtypeStruct((TILES, TILE), f32)


def first_meet(u, s, place, heat):
    return pl.pallas_call(
        first_body,
        out_shape=(jax.ShapeDtypeStruct((ROWS, FACES), bf16), FIELD, FIELD, ON_FACES),
        in_specs=[VMEM] * 4,
        out_specs=(VMEM,) * 4,
        scratch_shapes=scratch(3),
        compiler_params=params(40),
        name="first_meet",
    )(u, s, place, heat)


def later_meet(shift, u, s, place, diag, rows):
    return pl.pallas_call(
        functools.partial(later_body, shift),
        out_shape=(FIELD, ON_FACES),
        in_specs=[VMEM] * 5,
        out_specs=(VMEM,) * 2,
        scratch_shapes=scratch(2),
        compiler_params=params(40),
        name="later_meet",
    )(u, s, place, diag, rows)


def apply_body(step, *refs):
    (slots, reads, base, u, low_x, high_x, low_y, high_y, low_z, high_z) = refs[:10]
    (all_faces, factors, emissive, under, dots_in) = refs[10:15]
    older_u = refs[15 : 15 + step]
    older_s = refs[15 + step : 15 + 2 * step]
    s = refs[15 + 2 * step]
    outs = refs[16 + 2 * step :]
    last = step + 1 == ITERS
    if last:
        (dots_out,) = outs
    else:
        (u_out, s_out, dots_out, first_x, last_x, out_ly, out_hy, out_lz, out_hz) = outs
        out_lz[...] = jnp.zeros((CY, CZ), f32)
        out_hz[...] = jnp.zeros((CY, CZ), f32)
    shift = SHIFTS[step]
    lane = iota((CY, CZ), 1)
    sub = iota((CY, CZ), 0)

    def plane(x, before, after, sums):
        cur = u[x]
        beside = before + after
        beside = beside + jnp.where(sub == 0, low_y[pl.ds(x, 1), :], pltpu.roll(cur, 1, 0))
        beside = beside + jnp.where(
            sub == CY - 1, high_y[pl.ds(x, 1), :], pltpu.roll(cur, CY - 1, 0)
        )
        beside = beside + jnp.where(
            lane == 0, pltpu.roll(low_z[...], (CZ - x) % CZ, 1), pltpu.roll(cur, 1, 1)
        )
        beside = beside + jnp.where(
            lane == CZ - 1, pltpu.roll(high_z[...], CZ - 1 - x, 1), pltpu.roll(cur, CZ - 1, 1)
        )
        new = (base[x] - beside) * SCALE
        if not last:
            u_out[x] = new
            pack_edges(new, x, lane, out_ly, out_hy, out_lz, out_hz)
        against = [old[x] for old in older_u] + [cur, new]
        products = [new * other for other in against]
        if step == 0:
            products.append(cur * cur)
        return tuple(
            acc + (p[0:8] + p[8:16] + p[16:24] + p[24:32]) for acc, p in zip(sums, products)
        )

    count = step + 2 + (step == 0)
    sums = tuple(jnp.zeros((8, CZ), f32) for _ in range(count))
    sums = plane(0, low_x[...], u[1], sums)
    sums = lax.fori_loop(
        1, CX - 1, lambda x, c: plane(x, u[x - 1], u[x + 1], c), sums, unroll=2
    )
    sums = plane(CX - 1, u[CX - 2], high_x[...], sums)
    if not last:
        first_x[...] = u_out[0]
        last_x[...] = u_out[CX - 1]

    eye = iota((TILE, TILE), 0) == iota((TILE, TILE), 1)
    face_sums = [jnp.zeros((1, TILE), f32) for _ in range(count)]

    def tile(i, carry):
        acc = None
        for k in range(SLOTS):
            slot = slots[i * SLOTS + k]
            column = lax.shift_right_logical(slot, 2) * TILES + reads[slot]
            term = factors[i, k] * all_faces[pl.ds(column, 1), :]
            acc = term if acc is None else acc + term
        row = jnp.sum(acc, axis=1, keepdims=True)
        flux = jnp.sum(jnp.where(eye, row, 0.0), axis=0, keepdims=True)
        at = pl.ds(i, 1)
        own = s[at, :]
        e = emissive[at, :]
        new = ((1.0 - shift + e) * own - under[at, :] - e * flux) * SCALE
        if not last:
            s_out[at, :] = new
        against = [old[at, :] for old in older_s] + [own, new]
        products = [new * other for other in against]
        if step == 0:
            products.append(own * own)
        return tuple(c + p for c, p in zip(carry, products))

    face_sums = lax.fori_loop(0, TILES, tile, tuple(face_sums), unroll=2)
    spot = iota((1, CZ), 1)
    row = dots_in[...]
    start = (0, 3, 6)[step]
    for d in range(count):
        whole = jnp.sum(jnp.sum(sums[d], axis=0, keepdims=True) + face_sums[d])
        row = jnp.where(spot == start + d, whole, row)
    dots_out[...] = row


DOTS = jax.ShapeDtypeStruct((1, CZ), f32)
PLANE = jax.ShapeDtypeStruct((CY, CZ), f32)


def apply(step, slots, reads, base, u, halos, all_faces, factors, emissive, under, dots, old_u, old_s, s):
    outs = (DOTS,)
    if step + 1 < ITERS:
        outs = (jax.ShapeDtypeStruct((CX, CY, CZ), f32), ON_FACES, DOTS, PLANE, PLANE) + EDGE_SHAPES
    return pl.pallas_call(
        functools.partial(apply_body, step),
        out_shape=outs,
        in_specs=[SMEM, SMEM] + [VMEM] * (14 + 2 * step),
        out_specs=(VMEM,) * len(outs),
        compiler_params=params(32),
        name="apply_operator",
    )(slots, reads, base, u, *halos, all_faces, factors, emissive, under, dots, *old_u, *old_s, s)


def finish_body(parts, u0, u1, u2, s0, s1, s2, out_u, out_s):
    total = jnp.sum(parts[...], axis=0, keepdims=True)
    entry = [total[:, d : d + 1] for d in range(10)]
    (g01, g11, g00, g02, g12, g22, g03, g13, g23, g33) = entry
    gram = [
        [g00, g01, g02, g03],
        [g01, g11, g12, g13],
        [g02, g12, g22, g23],
        [g03, g13, g23, g33],
    ]
    grow = 1.0 / SCALE
    image = [
        [SHIFTS[j] * gram[j][b] + grow * gram[j + 1][b] for b in range(ITERS + 1)]
        for j in range(ITERS)
    ]
    normal = [
        [SHIFTS[b] * image[a][b] + grow * image[a][b + 1] for b in range(ITERS)]
        for a in range(ITERS)
    ]
    target = [image[a][0] for a in range(ITERS)]
    for col in range(ITERS):
        for row in range(col + 1, ITERS):
            factor = normal[row][col] / normal[col][col]
            normal[row] = [normal[row][b] - factor * normal[col][b] for b in range(ITERS)]
            target[row] = target[row] - factor * target[col]
    coeffs = [None] * ITERS
    for row in range(ITERS - 1, -1, -1):
        acc = target[row]
        for b in range(row + 1, ITERS):
            acc = acc - normal[row][b] * coeffs[b]
        coeffs[row] = acc / normal[row][row]
    wide = [jnp.broadcast_to(c, (TILES, TILE)) for c in coeffs]
    out_s[...] = wide[0] * s0[...] + wide[1] * s1[...] + wide[2] * s2[...]

    def rows(i, carry):
        at = pl.ds(pl.multiple_of(i * TILES, TILES), TILES)
        out_u[at, :] = wide[0] * u0[at, :] + wide[1] * u1[at, :] + wide[2] * u2[at, :]
        return carry

    lax.fori_loop(0, ROWS // TILES, rows, 0, unroll=8)


def finish(parts, fields, faces):
    return pl.pallas_call(
        finish_body,
        out_shape=(FIELD, ON_FACES),
        in_specs=[VMEM] * 7,
        out_specs=(VMEM,) * 2,
        compiler_params=params(16),
        name="finish",
    )(parts, *fields, *faces)


def shifted(x, axis, up):
    ends = lax.axis_size(axis) - 1
    pairs = [(i, i + 1) if up else (i + 1, i) for i in range(ends)]
    return lax.ppermute(x, axis, pairs)


def local(
    rhs_cells, heat_diag, rhs_faces, emissive, view_factors, tile_slots, read_lists, face_cells
):
    slab = ("gy", "gz")
    everyone = ("gx", "gy", "gz")
    group = lax.axis_size(slab)
    slots = tile_slots.reshape(-1)
    reads = read_lists.reshape(-1)
    flat = (ROWS, CZ)
    fields, faces = [rhs_cells], [rhs_faces]
    dots = jnp.zeros((1, CZ), f32)
    sides = (rhs_cells[0], rhs_cells[CX - 1]) + tuple(edges(rhs_cells))
    for j in range(ITERS):
        u, s = fields[j], faces[j]
        first_x, last_x, low_y, high_y, low_z, high_z = sides
        halos = (
            shifted(last_x, "gx", True),
            shifted(first_x, "gx", False),
            shifted(high_y, "gy", True),
            shifted(low_y, "gy", False),
            shifted(high_z, "gz", True),
            shifted(low_z, "gz", False),
        )
        sent = jnp.broadcast_to(s[None], (group,) + s.shape)
        all_faces = lax.all_to_all(sent, slab, 0, 0, tiled=True).reshape(-1, TILE)
        if j == 0:
            rows, diag, base, under = first_meet(
                u.reshape(flat), s, face_cells, heat_diag.reshape(flat)
            )
        else:
            base, under = later_meet(SHIFTS[j], u.reshape(flat), s, face_cells, diag, rows)
        outs = apply(
            j, slots, reads, base.reshape(CX, CY, CZ), u, halos, all_faces, view_factors,
            emissive, under, dots, fields[:j], faces[:j], s,
        )
        if j + 1 < ITERS:
            fields.append(outs[0])
            faces.append(outs[1])
            dots = outs[2]
            sides = outs[3:]
        else:
            dots = outs[0]
    devices = lax.axis_size(everyone)
    parts = lax.all_to_all(
        jnp.broadcast_to(dots[None], (devices, 1, CZ)), everyone, 0, 0, tiled=True
    )
    sol_cells, sol_faces = finish(
        parts.reshape(devices, CZ), [u.reshape(flat) for u in fields], faces
    )
    return (sol_cells.reshape(CX, CY, CZ), sol_faces)


def solution(mesh):
    placed = (
        P("gx", "gy", "gz"),
        P("gx", "gy", "gz"),
        P(("gx", "gy", "gz"), None),
        P(("gx", "gy", "gz"), None),
        P(("gx", "gy", "gz"), None, None, None),
        P(("gx", "gy", "gz"), None),
        P(("gx", "gy", "gz"), None, None),
        P(("gx", "gy", "gz"), None),
    )
    return jax.shard_map(
        local,
        mesh=mesh,
        in_specs=placed,
        out_specs=(P("gx", "gy", "gz"), P(("gx", "gy", "gz"), None)),
        check_vma=False,
    )
```

```python
import functools

import jax
import jax.numpy as jnp
from jax import lax
from jax.experimental import pallas as pl
from jax.experimental.pallas import tpu as pltpu
from jax.sharding import PartitionSpec as P

ITERS = 3
SHIFTS = (6.0, 3.0, 11.0)
SCALE = 0.125
CX, CY, CZ = 64, 32, 128
ROWS = CX * CY
TILES = 16
TILE = 128
FACES = TILES * TILE
SLOTS = 4
PER_OWNER = 4
f32 = jnp.float32
bf16 = jnp.bfloat16
VMEM = pl.BlockSpec(memory_space=pltpu.VMEM)
SMEM = pl.BlockSpec(memory_space=pltpu.SMEM)
HBM = pl.BlockSpec(memory_space=pltpu.HBM)
AXES = ("gx", "gy", "gz")
FIELD = jax.ShapeDtypeStruct((ROWS, CZ), f32)
ON_FACES = jax.ShapeDtypeStruct((TILES, TILE), f32)
ONE_HOT = jax.ShapeDtypeStruct((ROWS, FACES), bf16)
SIDE = ((CY, CZ), (CX, CZ), (TILES, TILE))
SIDES = tuple(jax.ShapeDtypeStruct(shape, f32) for shape in SIDE for _ in range(2))


def params(mib):
    return pltpu.CompilerParams(vmem_limit_bytes=mib << 20)


def split(x):
    high = x.astype(bf16)
    return high, (x - high.astype(f32)).astype(bf16)


def iota(shape, dim):
    return lax.broadcasted_iota(jnp.int32, shape, dim)


class Copies:
    def __init__(self, sems):
        self.sems = sems
        self.used = 0

    def start(self, source, target):
        copy = pltpu.make_async_copy(source, target, self.sems.at[self.used])
        self.used += 1
        copy.start()
        return copy


def outward(axis):
    odd = lax.rem(lax.axis_index(axis), 2)
    return 1 - odd, odd


def send_sides(copies, cells, edge_y, edge_z, sides):
    started = []
    for side, out in zip(outward("gx"), sides[0:2]):
        started.append(copies.start(cells.at[pl.ds(side * (ROWS - CY), CY), :], out))
    for edge, axis, outs in ((edge_y, "gy", sides[2:4]), (edge_z, "gz", sides[4:6])):
        for side, out in zip(outward(axis), outs):
            started.append(copies.start(edge.at[side], out))
    return started


def turn(u, edge_z, wide):
    for i in range(TILES):
        at = pl.ds(i * TILE, TILE)
        part = u[at, :].T
        edge_z[0, i : i + 1, :] = part[0:1, :]
        edge_z[1, i : i + 1, :] = part[CZ - 1 : CZ, :]
        high, low = split(part)
        wide[0:CZ, at] = high
        wide[CZ : 2 * CZ, at] = low


def meet(s, rows, place, count, spread, wide, under):
    z = iota((CZ, TILE), 0)
    for i in range(TILES):
        at = pl.ds(i * TILE, TILE)
        here = z == (place[i : i + 1, :] & (CZ - 1))
        high, low = split(s[i : i + 1, :])
        spread[0:CZ, at] = jnp.where(here, high.astype(f32), 0.0).astype(bf16)
        spread[CZ : 2 * CZ, at] = jnp.where(here, low.astype(f32), 0.0).astype(bf16)
        if count:
            spread[2 * CZ : 3 * CZ, at] = jnp.where(here, 1.0, 0.0).astype(bf16)
    seen = jnp.dot(wide[...], rows[...], preferred_element_type=f32)
    for i in range(TILES):
        here = z == (place[i : i + 1, :] & (CZ - 1))
        at = slice(i * TILE, (i + 1) * TILE)
        both = seen[0:CZ, at] + seen[CZ : 2 * CZ, at]
        under[i : i + 1, :] = jnp.sum(jnp.where(here, both, 0.0), axis=0, keepdims=True)
    return lax.dot_general(
        rows[...], spread[...], (((1,), (1,)), ((), ())), preferred_element_type=f32
    )


def first_body(*refs):
    (u_in, s_in, place_in, heat_in) = refs[:4]
    (rows_out, diag_out, base_out, under_out) = refs[4:8]
    sides = refs[8:14]
    (u, s, place, heat, rows, base, under, edge_y, edge_z, spread, wide, sems) = refs[14:]
    copies = Copies(sems)
    get_place = copies.start(place_in, place)
    get_u = copies.start(u_in, u)
    get_s = copies.start(s_in, s)
    get_heat = copies.start(heat_in, heat)
    get_place.wait()
    number = iota((ROWS, TILE), 0)
    for i in range(TILES):
        row = lax.shift_right_logical(place[i : i + 1, :], 7)
        rows[:, pl.ds(i * TILE, TILE)] = jnp.where(number == row, 1.0, 0.0).astype(bf16)
    puts = [copies.start(rows, rows_out)]
    get_u.wait()
    for x in range(CX):
        edge_y[0, x : x + 1, :] = u[x * CY : x * CY + 1, :]
        edge_y[1, x : x + 1, :] = u[(x + 1) * CY - 1 : (x + 1) * CY, :]
    turn(u, edge_z, wide)
    puts += send_sides(copies, u, edge_y, edge_z, sides)
    get_s.wait()
    sums = meet(s, rows, place, True, spread, wide, under)
    puts.append(copies.start(under, under_out))
    get_heat.wait()
    total = 6.0 + heat[...] + sums[:, 2 * CZ : 3 * CZ]
    heat[...] = total
    base[...] = (total - SHIFTS[0]) * u[...] - (sums[:, 0:CZ] + sums[:, CZ : 2 * CZ])
    puts.append(copies.start(heat, diag_out))
    puts.append(copies.start(base, base_out))
    for put in puts:
        put.wait()


def field():
    return pltpu.VMEM((ROWS, CZ), f32)


def on_faces(dtype=f32):
    return pltpu.VMEM((TILES, TILE), dtype)


def one_hot():
    return pltpu.VMEM((ROWS, FACES), bf16)


def edge_buffers():
    return [pltpu.VMEM((2, CX, CZ), f32), pltpu.VMEM((2, TILES, TILE), f32)]


def first(u, s, place, heat):
    scratch = [field(), on_faces(), on_faces(jnp.int32), field(), one_hot(), field(), on_faces()]
    scratch += edge_buffers()
    scratch += [pltpu.VMEM((3 * CZ, FACES), bf16), pltpu.VMEM((2 * CZ, FACES), bf16)]
    scratch += [pltpu.SemaphoreType.DMA((14,))]
    outs = (ONE_HOT, FIELD, FIELD, ON_FACES) + SIDES
    return pl.pallas_call(
        first_body,
        out_shape=outs,
        in_specs=[HBM] * 4,
        out_specs=(HBM,) * len(outs),
        scratch_shapes=scratch,
        compiler_params=params(64),
        name="first_meet",
    )(u, s, place, heat)


def stencil(step, u, base, edge_y, edge_z, new_rows, sums):
    sub = iota((CY, CZ), 0)
    lane = iota((CY, CZ), 1)
    z = iota((CZ, TILE), 0)

    def block(i, sums):
        at_z = pl.ds(i, 1)
        facing = jnp.where(z == 0, edge_z[0, at_z, :], 0.0)
        facing = jnp.where(z == CZ - 1, edge_z[1, at_z, :], facing).T
        for q in range(4):
            x = i * 4 + q
            row = pl.multiple_of(x * CY, CY)
            cur = u[pl.ds(row + CY, CY), :]
            beside = u[pl.ds(row, CY), :] + u[pl.ds(row + 2 * CY, CY), :]
            at_y = pl.ds(x, 1)
            low = jnp.where(sub == 0, edge_y[0, at_y, :], pltpu.roll(cur, 1, 0))
            high = jnp.where(sub == CY - 1, edge_y[1, at_y, :], pltpu.roll(cur, CY - 1, 0))
            beside = beside + (low + high)
            low = jnp.where(lane == 0, 0.0, pltpu.roll(cur, 1, 1))
            high = jnp.where(lane == CZ - 1, 0.0, pltpu.roll(cur, CZ - 1, 1))
            beside = beside + (low + high) + facing[q * CY : (q + 1) * CY, :]
            new = (base[pl.ds(row, CY), :] - beside) * SCALE
            sums = new_rows(x, row, cur, new, sums)
        return sums

    return lax.fori_loop(0, TILES, block, sums, unroll=2)


def emission(step, slots, reads, factors, all_faces, emissive, own, under, new_faces, sums):
    eye = iota((TILE, TILE), 0) == iota((TILE, TILE), 1)

    def tile(i, sums):
        acc = None
        for k in range(SLOTS):
            slot = slots[i * SLOTS + k]
            column = lax.shift_right_logical(slot, 2) * TILES + reads[slot]
            term = factors[i, k] * all_faces[pl.ds(column, 1), :]
            acc = term if acc is None else acc + term
        row = jnp.sum(acc, axis=1, keepdims=True)
        flux = jnp.sum(jnp.where(eye, row, 0.0), axis=0, keepdims=True)
        at = pl.ds(i, 1)
        mine = own[at, :]
        e = emissive[at, :]
        new = ((1.0 - SHIFTS[step] + e) * mine - under[at, :] - e * flux) * SCALE
        return new_faces(at, mine, new, sums)

    return lax.fori_loop(0, TILES, tile, sums, unroll=4)


def get_halos(copies, halos, u, edge_y, edge_z):
    started = []
    for side, halo in zip(outward("gx"), halos[0:2]):
        started.append(copies.start(halo, u.at[pl.ds(side * (ROWS + CY), CY), :]))
    for edge, axis, pair in ((edge_y, "gy", halos[2:4]), (edge_z, "gz", halos[4:6])):
        for side, halo in zip(outward(axis), pair):
            started.append(copies.start(halo, edge.at[side]))
    return started


def wait_all(copies):
    for copy in copies:
        copy.wait()


def middle_body(step, *refs):
    (slots, reads, u_in, base_in, all_in, factors_in, emissive_in, under_in, s_in) = refs[:9]
    (place_in, diag_in, rows_in) = refs[9:12]
    halos = refs[12:18]
    (u_out, s_out, base_out, under_out) = refs[18:22]
    sides = refs[22:28]
    (u, base, all_faces, factors, emissive, under, s, place, diag, rows) = refs[28:38]
    (new_u, new_s, halo_y, halo_z, edge_y, edge_z, spread, wide, sems) = refs[38:]
    copies = Copies(sems)
    cells = [copies.start(u_in, u.at[pl.ds(CY, ROWS), :]), copies.start(base_in, base)]
    cells += get_halos(copies, halos, u, halo_y, halo_z)
    pairs = ((all_in, all_faces), (emissive_in, emissive), (under_in, under), (s_in, s))
    faces = [copies.start(a, b) for a, b in pairs + ((factors_in, factors),)]
    pairs = ((place_in, place), (rows_in, rows), (diag_in, diag))
    rest = [copies.start(a, b) for a, b in pairs]
    wait_all(cells)

    def new_rows(x, row, cur, new, sums):
        new_u[pl.ds(row, CY), :] = new
        edge_y[0, pl.ds(x, 1), :] = new[0:1, :]
        edge_y[1, pl.ds(x, 1), :] = new[CY - 1 : CY, :]
        return sums

    def new_faces(at, mine, new, sums):
        new_s[at, :] = new
        return sums

    stencil(step, u, base, halo_y, halo_z, new_rows, 0)
    puts = [copies.start(new_u, u_out)]
    wait_all(faces)
    emission(step, slots, reads, factors, all_faces, emissive, s, under, new_faces, 0)
    puts.append(copies.start(new_s, s_out))
    turn(new_u, edge_z, wide)
    puts += send_sides(copies, new_u, edge_y, edge_z, sides)
    wait_all(rest)
    sums = meet(new_s, rows, place, False, spread, wide, under)
    puts.append(copies.start(under, under_out))
    base[...] = (diag[...] - SHIFTS[step + 1]) * new_u[...] - (
        sums[:, 0:CZ] + sums[:, CZ : 2 * CZ]
    )
    puts.append(copies.start(base, base_out))
    wait_all(puts)


def middle(step, slots, reads, u, base, all_faces, factors, emissive, under, s, place, diag, rows, halos):
    scratch = [
        pltpu.VMEM((ROWS + 2 * CY, CZ), f32),
        field(),
        pltpu.VMEM(all_faces.shape, f32),
        pltpu.VMEM(factors.shape, f32),
        on_faces(),
        on_faces(),
        on_faces(),
        on_faces(jnp.int32),
        field(),
        one_hot(),
        field(),
        on_faces(),
    ]
    scratch += edge_buffers() + edge_buffers()
    scratch += [pltpu.VMEM((2 * CZ, FACES), bf16), pltpu.VMEM((2 * CZ, FACES), bf16)]
    scratch += [pltpu.SemaphoreType.DMA((26,))]
    outs = (FIELD, ON_FACES, FIELD, ON_FACES) + SIDES
    return pl.pallas_call(
        functools.partial(middle_body, step),
        out_shape=outs,
        in_specs=[SMEM, SMEM] + [HBM] * 16,
        out_specs=(HBM,) * len(outs),
        scratch_shapes=scratch,
        compiler_params=params(64),
        name="apply_and_meet",
    )(slots, reads, u, base, all_faces, factors, emissive, under, s, place, diag, rows, *halos)


def products(vectors):
    return [vectors[a] * vectors[b] for b in range(ITERS + 1) for a in range(b + 1)]


PAIRS = (ITERS + 1) * (ITERS + 2) // 2


def last_body(*refs):
    (slots, reads, u_in, base_in, all_in, factors_in, emissive_in, under_in, s_in) = refs[:9]
    (u0_in, u1_in, s0_in, s1_in) = refs[9:13]
    halos = refs[13:19]
    dots_out = refs[19]
    (u, base, all_faces, factors, emissive, under, s, u0, u1, s0, s1) = refs[20:31]
    (halo_y, halo_z, sems) = refs[31:]
    copies = Copies(sems)
    cells = [copies.start(u_in, u.at[pl.ds(CY, ROWS), :]), copies.start(base_in, base)]
    cells += get_halos(copies, halos, u, halo_y, halo_z)
    cells += [copies.start(u0_in, u0), copies.start(u1_in, u1)]
    pairs = ((all_in, all_faces), (emissive_in, emissive), (under_in, under), (s_in, s))
    pairs += ((s0_in, s0), (s1_in, s1), (factors_in, factors))
    faces = [copies.start(a, b) for a, b in pairs]
    wait_all(cells)

    def new_rows(x, row, cur, new, sums):
        at = pl.ds(row, CY)
        terms = products([u0[at, :], u1[at, :], cur, new])
        return tuple(
            acc + ((p[0:8] + p[8:16]) + (p[16:24] + p[24:32])) for acc, p in zip(sums, terms)
        )

    def new_faces(at, mine, new, sums):
        terms = products([s0[at, :], s1[at, :], mine, new])
        return tuple(acc + p for acc, p in zip(sums, terms))

    zeros = tuple(jnp.zeros((8, CZ), f32) for _ in range(PAIRS))
    by_cells = stencil(ITERS - 1, u, base, halo_y, halo_z, new_rows, zeros)
    wait_all(faces)
    zeros = tuple(jnp.zeros((1, TILE), f32) for _ in range(PAIRS))
    by_faces = emission(
        ITERS - 1, slots, reads, factors, all_faces, emissive, s, under, new_faces, zeros
    )
    spot = iota((1, CZ), 1)
    row = jnp.zeros((1, CZ), f32)
    for d in range(PAIRS):
        both = jnp.sum(by_cells[d], axis=0, keepdims=True) + by_faces[d]
        row = jnp.where(spot == d, jnp.sum(both, axis=1, keepdims=True), row)
    dots_out[...] = row


def last(slots, reads, u, base, all_faces, factors, emissive, under, s, u0, u1, s0, s1, halos):
    scratch = [
        pltpu.VMEM((ROWS + 2 * CY, CZ), f32),
        field(),
        pltpu.VMEM(all_faces.shape, f32),
        pltpu.VMEM(factors.shape, f32),
        on_faces(),
        on_faces(),
        on_faces(),
        field(),
        field(),
        on_faces(),
        on_faces(),
    ]
    scratch += edge_buffers()
    scratch += [pltpu.SemaphoreType.DMA((17,))]
    return pl.pallas_call(
        last_body,
        out_shape=jax.ShapeDtypeStruct((1, CZ), f32),
        in_specs=[SMEM, SMEM] + [HBM] * 17,
        out_specs=VMEM,
        scratch_shapes=scratch,
        compiler_params=params(64),
        name="apply_and_reduce",
    )(slots, reads, u, base, all_faces, factors, emissive, under, s, u0, u1, s0, s1, *halos)


def finish_body(parts, u0, u1, u2, s0, s1, s2, out_u, out_s):
    total = jnp.sum(parts[...], axis=0, keepdims=True)
    entry = [total[:, d : d + 1] for d in range(10)]
    (g00, g01, g11, g02, g12, g22, g03, g13, g23, g33) = entry
    gram = [
        [g00, g01, g02, g03],
        [g01, g11, g12, g13],
        [g02, g12, g22, g23],
        [g03, g13, g23, g33],
    ]
    grow = 1.0 / SCALE
    image = [
        [SHIFTS[j] * gram[j][b] + grow * gram[j + 1][b] for b in range(ITERS + 1)]
        for j in range(ITERS)
    ]
    normal = [
        [SHIFTS[b] * image[a][b] + grow * image[a][b + 1] for b in range(ITERS)]
        for a in range(ITERS)
    ]
    target = [image[a][0] for a in range(ITERS)]
    for col in range(ITERS):
        for row in range(col + 1, ITERS):
            factor = normal[row][col] / normal[col][col]
            normal[row] = [normal[row][b] - factor * normal[col][b] for b in range(ITERS)]
            target[row] = target[row] - factor * target[col]
    coeffs = [None] * ITERS
    for row in range(ITERS - 1, -1, -1):
        acc = target[row]
        for b in range(row + 1, ITERS):
            acc = acc - normal[row][b] * coeffs[b]
        coeffs[row] = acc / normal[row][row]
    wide = [jnp.broadcast_to(c, (TILES, TILE)) for c in coeffs]
    out_s[...] = wide[0] * s0[...] + wide[1] * s1[...] + wide[2] * s2[...]

    def rows(i, carry):
        at = pl.ds(pl.multiple_of(i * TILES, TILES), TILES)
        out_u[at, :] = wide[0] * u0[at, :] + wide[1] * u1[at, :] + wide[2] * u2[at, :]
        return carry

    lax.fori_loop(0, ROWS // TILES, rows, 0, unroll=8)


def finish(parts, fields, faces):
    return pl.pallas_call(
        finish_body,
        out_shape=(FIELD, ON_FACES),
        in_specs=[VMEM] * 7,
        out_specs=(VMEM,) * 2,
        compiler_params=params(64),
        name="finish",
    )(parts, *fields, *faces)


def exchanged(sides):
    halos = []
    for axis, pair in zip(AXES, (sides[0:2], sides[2:4], sides[4:6])):
        size = lax.axis_size(axis)
        even = [(i, i ^ 1) for i in range(size)]
        odd = [(i, i + 1) for i in range(1, size - 1, 2)]
        odd += [(b, a) for a, b in odd]
        halos += [lax.ppermute(pair[0], axis, even), lax.ppermute(pair[1], axis, odd)]
    return halos


def local(
    rhs_cells, heat_diag, rhs_faces, emissive, view_factors, tile_slots, read_lists, face_cells
):
    slab = ("gy", "gz")
    group = lax.axis_size(slab)
    devices = lax.axis_size(AXES)
    slots = tile_slots.reshape(-1)
    reads = read_lists.reshape(-1)
    flat = (ROWS, CZ)
    fields, faces = [rhs_cells.reshape(flat)], [rhs_faces]
    for j in range(ITERS):
        u, s = fields[j], faces[j]
        sent = jnp.broadcast_to(s[None], (group,) + s.shape)
        all_faces = lax.all_to_all(sent, slab, 0, 0, tiled=True).reshape(-1, TILE)
        if j == 0:
            rows, diag, base, under, *sides = first(u, s, face_cells, heat_diag.reshape(flat))
        halos = exchanged(sides)
        given = (slots, reads, u, base, all_faces, view_factors, emissive, under, s)
        if j + 1 < ITERS:
            u, s, base, under, *sides = middle(j, *given, face_cells, diag, rows, halos)
            fields.append(u)
            faces.append(s)
        else:
            dots = last(*given, *fields[:j], *faces[:j], halos)
    parts = lax.all_to_all(
        jnp.broadcast_to(dots[None], (devices, 1, CZ)), AXES, 0, 0, tiled=True
    )
    sol_cells, sol_faces = finish(parts.reshape(devices, CZ), fields, faces)
    return (sol_cells.reshape(CX, CY, CZ), sol_faces)


def solution(mesh):
    placed = (
        P("gx", "gy", "gz"),
        P("gx", "gy", "gz"),
        P(("gx", "gy", "gz"), None),
        P(("gx", "gy", "gz"), None),
        P(("gx", "gy", "gz"), None, None, None),
        P(("gx", "gy", "gz"), None),
        P(("gx", "gy", "gz"), None, None),
        P(("gx", "gy", "gz"), None),
    )
    return jax.shard_map(
        local,
        mesh=mesh,
        in_specs=placed,
        out_specs=(P("gx", "gy", "gz"), P(("gx", "gy", "gz"), None)),
        check_vma=False,
    )
```

```python
import functools

import jax
import jax.numpy as jnp
from jax import lax
from jax.experimental import pallas as pl
from jax.experimental.pallas import tpu as pltpu
from jax.sharding import PartitionSpec as P

ITERS = 3
SHIFTS = (6.0, 3.0, 11.0)
SCALE = 0.125
CX, CY, CZ = 64, 32, 128
ROWS = CX * CY
TILES = 16
TILE = 128
FACES = TILES * TILE
SLOTS = 4
PER_OWNER = 4
f32 = jnp.float32
bf16 = jnp.bfloat16
VMEM = pl.BlockSpec(memory_space=pltpu.VMEM)
SMEM = pl.BlockSpec(memory_space=pltpu.SMEM)
HBM = pl.BlockSpec(memory_space=pltpu.HBM)
AXES = ("gx", "gy", "gz")
FIELD = jax.ShapeDtypeStruct((ROWS, CZ), f32)
ON_FACES = jax.ShapeDtypeStruct((TILES, TILE), f32)
CHUNKS = 4
PART = ROWS // CHUNKS
SIDE = ((CY, CZ), (CX, CZ), (TILES, TILE))
SIDES = tuple(jax.ShapeDtypeStruct(shape, f32) for shape in SIDE for _ in range(2))


def params(mib):
    return pltpu.CompilerParams(vmem_limit_bytes=mib << 20)


def split(x):
    high = x.astype(bf16)
    return high, (x - high.astype(f32)).astype(bf16)


def iota(shape, dim):
    return lax.broadcasted_iota(jnp.int32, shape, dim)


class Copies:
    def __init__(self, sems):
        self.sems = sems
        self.used = 0

    def start(self, source, target):
        copy = pltpu.make_async_copy(source, target, self.sems.at[self.used])
        self.used += 1
        copy.start()
        return copy


def outward(axis):
    odd = lax.rem(lax.axis_index(axis), 2)
    return 1 - odd, odd


def send_sides(copies, cells, edge_y, edge_z, sides):
    started = []
    for side, out in zip(outward("gx"), sides[0:2]):
        started.append(copies.start(cells.at[pl.ds(side * (ROWS - CY), CY), :], out))
    for edge, axis, outs in ((edge_y, "gy", sides[2:4]), (edge_z, "gz", sides[4:6])):
        for side, out in zip(outward(axis), outs):
            started.append(copies.start(edge.at[side], out))
    return started


def mark(rows, place):
    number = iota((ROWS, TILE), 0).astype(jnp.int16)
    one = jnp.ones((ROWS, TILE), bf16)
    zero = jnp.zeros((ROWS, TILE), bf16)

    def tile(i, carry):
        row = lax.shift_right_logical(place[pl.ds(i, 1), :], 7)
        row = jnp.broadcast_to(row, (16, TILE)).astype(jnp.int16)
        row = jnp.concatenate([row] * (ROWS // 16), axis=0)
        at = pl.ds(pl.multiple_of(i * TILE, TILE), TILE)
        rows[:, at] = jnp.where(number == row, one, zero)
        return carry

    lax.fori_loop(0, TILES, tile, 0)


def turn(u, wide, edge_z=None):
    def tile(i, carry):
        at = pl.ds(pl.multiple_of(i * TILE, TILE), TILE)
        part = u[at, :].T
        if edge_z is not None:
            edge_z[0, pl.ds(i, 1), :] = part[0:1, :]
            edge_z[1, pl.ds(i, 1), :] = part[CZ - 1 : CZ, :]
        high, low = split(part)
        wide[0:CZ, at] = high
        wide[CZ : 2 * CZ, at] = low
        return carry

    lax.fori_loop(0, TILES, tile, 0, unroll=4)


def look(rows, place, wide, under):
    z = iota((CZ, TILE), 0)
    width = TILES // CHUNKS
    for c in range(CHUNKS):
        at = slice(c * width * TILE, (c + 1) * width * TILE)
        seen = jnp.dot(wide[...], rows[:, at], preferred_element_type=f32)
        both = seen[0:CZ] + seen[CZ : 2 * CZ]
        for h in range(width):
            i = c * width + h
            here = z == (place[i : i + 1, :] & (CZ - 1))
            part = jnp.where(here, both[:, h * TILE : (h + 1) * TILE], 0.0)
            under[i : i + 1, :] = jnp.sum(part, axis=0, keepdims=True)


def lay(s, under, place, spread):
    z = iota((CZ, TILE), 0)

    def tile(i, carry):
        at = pl.ds(pl.multiple_of(i * TILE, TILE), TILE)
        here = z == (place[pl.ds(i, 1), :] & (CZ - 1))
        high, low = split(1.0 * (under[pl.ds(i, 1), :] - s[pl.ds(i, 1), :]))
        spread[0:CZ, at] = jnp.where(here, high.astype(f32), 0.0).astype(bf16)
        spread[CZ : 2 * CZ, at] = jnp.where(here, low.astype(f32), 0.0).astype(bf16)
        return carry

    lax.fori_loop(0, TILES, tile, 0, unroll=4)


def meet(copies, shift, u, s, rows, place, heat, spread, wide, under, base_out, under_out):
    look(rows, place, wide, under)
    puts = [copies.start(under, under_out)]
    lay(s, under, place, spread)
    for c in range(CHUNKS):
        at = pl.ds(c * PART, PART)
        sums = lax.dot_general(
            rows[at, :], spread[...], (((1,), (1,)), ((), ())), preferred_element_type=f32
        )
        heat[at, :] = (heat[at, :] + (6.0 - shift)) * u[at, :] + (
            sums[:, 0:CZ] + sums[:, CZ : 2 * CZ]
        )
        puts.append(copies.start(heat.at[at], base_out.at[at]))
    return puts


def wait_all(copies):
    for copy in copies:
        copy.wait()


def first_body(*refs):
    (u_in, s_in, place_in, heat_in, base_out, under_out) = refs[:6]
    sides = refs[6:12]
    (u, s, place, heat, rows, under, edge_y, edge_z, spread, wide, sems) = refs[12:]
    copies = Copies(sems)
    get_place = copies.start(place_in, place)
    get_u = copies.start(u_in, u)
    rest = [copies.start(s_in, s), copies.start(heat_in, heat)]
    get_place.wait()
    mark(rows, place)
    get_u.wait()
    for x in range(CX):
        edge_y[0, x : x + 1, :] = u[x * CY : x * CY + 1, :]
        edge_y[1, x : x + 1, :] = u[(x + 1) * CY - 1 : (x + 1) * CY, :]
    turn(u, wide, edge_z)
    puts = send_sides(copies, u, edge_y, edge_z, sides)
    wait_all(rest)
    puts += meet(
        copies, SHIFTS[0], u, s, rows, place, heat, spread, wide, under, base_out, under_out
    )
    wait_all(puts)


def field():
    return pltpu.VMEM((ROWS, CZ), f32)


def on_faces(dtype=f32):
    return pltpu.VMEM((TILES, TILE), dtype)


def one_hot():
    return pltpu.VMEM((ROWS, FACES), bf16)


def edge_buffers():
    return [pltpu.VMEM((2, CX, CZ), f32), pltpu.VMEM((2, TILES, TILE), f32)]


def call(body, name, ins, outs, scratch, sems, smem=0):
    specs = [SMEM] * smem + [HBM] * (len(ins) - smem)
    return pl.pallas_call(
        body,
        out_shape=tuple(outs),
        in_specs=specs,
        out_specs=(HBM,) * len(outs),
        scratch_shapes=list(scratch) + [pltpu.SemaphoreType.DMA((sems,))],
        compiler_params=params(64),
        name=name,
    )(*ins)


def parts():
    return [pltpu.VMEM((2 * CZ, FACES), bf16), pltpu.VMEM((2 * CZ, FACES), bf16)]


def first(u, s, place, heat):
    scratch = [field(), on_faces(), on_faces(jnp.int32), field(), one_hot(), on_faces()]
    scratch += edge_buffers() + parts()
    return call(
        first_body, "first_meet", (u, s, place, heat), (FIELD, ON_FACES) + SIDES, scratch, 15
    )


def stencil(step, chunk, u, base, edge_y, edge_z, new_block, sums):
    sub = iota((CY, CZ), 0)
    lane = iota((CY, CZ), 1)
    z = iota((CZ, TILE), 0)

    def block(i, sums):
        at_z = pl.ds(i, 1)
        facing = jnp.where(z == 0, edge_z[0, at_z, :], 0.0)
        facing = jnp.where(z == CZ - 1, edge_z[1, at_z, :], facing).T
        made = []
        for q in range(4):
            x = i * 4 + q
            row = pl.multiple_of(x * CY, CY)
            cur = u[pl.ds(row + CY, CY), :]
            beside = u[pl.ds(row, CY), :] + u[pl.ds(row + 2 * CY, CY), :]
            at_y = pl.ds(x, 1)
            low = jnp.where(sub == 0, edge_y[0, at_y, :], pltpu.roll(cur, 1, 0))
            high = jnp.where(sub == CY - 1, edge_y[1, at_y, :], pltpu.roll(cur, CY - 1, 0))
            beside = beside + (low + high)
            low = jnp.where(lane == 0, 0.0, pltpu.roll(cur, 1, 1))
            high = jnp.where(lane == CZ - 1, 0.0, pltpu.roll(cur, CZ - 1, 1))
            beside = beside + (low + high) + facing[q * CY : (q + 1) * CY, :]
            made.append((cur, (base[pl.ds(row, CY), :] - beside) * SCALE))
        return new_block(i, made, sums)

    count = TILES // CHUNKS
    return lax.fori_loop(chunk * count, (chunk + 1) * count, block, sums, unroll=2)


def emission(step, chunk, slots, reads, factors, all_faces, emissive, own, under, new_faces, sums):
    eye = iota((TILE, TILE), 0) == iota((TILE, TILE), 1)

    def tile(i, sums):
        acc = None
        for k in range(SLOTS):
            slot = slots[k, i]
            owner = lax.shift_right_logical(slot, 2)
            column = owner * TILES + reads[slot & (PER_OWNER - 1), owner]
            term = factors[i, k] * all_faces[pl.ds(column, 1), :]
            acc = term if acc is None else acc + term
        row = jnp.sum(acc, axis=1, keepdims=True)
        flux = jnp.sum(jnp.where(eye, row, 0.0), axis=0, keepdims=True)
        at = pl.ds(i, 1)
        mine = own[at, :]
        e = emissive[at, :]
        new = ((1.0 - SHIFTS[step] + e) * mine - under[at, :] - e * flux) * SCALE
        return new_faces(at, mine, new, sums)

    count = TILES // CHUNKS
    return lax.fori_loop(chunk * count, (chunk + 1) * count, tile, sums, unroll=count)


def get_halos(copies, halos, u, edge_y, edge_z):
    started = []
    for side, halo in zip(outward("gx"), halos[0:2]):
        started.append(copies.start(halo, u.at[pl.ds(side * (ROWS + CY), CY), :]))
    for edge, axis, pair in ((edge_y, "gy", halos[2:4]), (edge_z, "gz", halos[4:6])):
        for side, halo in zip(outward(axis), pair):
            started.append(copies.start(halo, edge.at[side]))
    return started


def in_chunks(copies, source, target, offset=0):
    part = source.shape[0] // CHUNKS
    return [
        copies.start(source.at[pl.ds(c * part, part)], target.at[pl.ds(offset + c * part, part)])
        for c in range(CHUNKS)
    ]


def cells_body(step, *refs):
    (u_in, base_in, s_in, place_in, heat_in) = refs[:5]
    halos = refs[5:11]
    (u_out, base_out, under_out) = refs[11:14]
    sides = refs[14:20]
    (u, base, s, place, heat, new_u, halo_y, halo_z, edge_y, edge_z) = refs[20:30]
    (rows, under, spread, wide, sems) = refs[30:]
    copies = Copies(sems)
    get_place = copies.start(place_in, place)
    get_u = in_chunks(copies, u_in, u, CY)
    gets = get_halos(copies, halos, u, halo_y, halo_z)
    get_base = in_chunks(copies, base_in, base)
    rest = [copies.start(s_in, s), copies.start(heat_in, heat)]
    get_place.wait()
    mark(rows, place)
    wait_all(get_u + gets)

    def new_block(i, made, sums):
        for q, (_, new) in enumerate(made):
            new_u[pl.ds(pl.multiple_of(i * TILE + q * CY, CY), CY), :] = new
            edge_y[0, pl.ds(i * 4 + q, 1), :] = new[0:1, :]
            edge_y[1, pl.ds(i * 4 + q, 1), :] = new[CY - 1 : CY, :]
        return sums

    puts = []
    for c in range(CHUNKS):
        get_base[c].wait()
        stencil(step, c, u, base, halo_y, halo_z, new_block, 0)
        at = pl.ds(c * PART, PART)
        puts.append(copies.start(new_u.at[at], u_out.at[at]))
    turn(new_u, wide, edge_z)
    puts += send_sides(copies, new_u, edge_y, edge_z, sides)
    wait_all(rest)
    puts += meet(
        copies, SHIFTS[step + 1], new_u, s, rows, place, heat, spread, wide, under,
        base_out, under_out,
    )
    wait_all(puts)


def cells(step, u, base, s, place, heat, halos):
    scratch = [pltpu.VMEM((ROWS + 2 * CY, CZ), f32), field(), on_faces(), on_faces(jnp.int32)]
    scratch += [field(), field()] + edge_buffers() + edge_buffers()
    scratch += [one_hot(), on_faces()] + parts()
    body = functools.partial(cells_body, step)
    outs = (FIELD, FIELD, ON_FACES) + SIDES
    return call(body, "cells_step", (u, base, s, place, heat, *halos), outs, scratch, 32)


def faces_body(step, *refs):
    (slots, reads, all_in, factors_in, emissive_in, under_in, s_in, s_out, sent_out) = refs[:9]
    (all_faces, factors, emissive, under, s, new_s, sent, sems) = refs[9:]
    copies = Copies(sems)
    pairs = ((all_in, all_faces), (emissive_in, emissive), (under_in, under), (s_in, s))
    gets = [copies.start(a, b) for a, b in pairs]
    get_factors = in_chunks(copies, factors_in, factors)
    wait_all(gets)

    def new_faces(at, mine, new, sums):
        new_s[at, :] = new
        return sums

    for c in range(CHUNKS):
        get_factors[c].wait()
        emission(step, c, slots, reads, factors, all_faces, emissive, s, under, new_faces, 0)
    puts = [copies.start(new_s, s_out)]
    value = new_s[...]
    for q in range(sent.shape[0]):
        sent[q] = value
    puts.append(copies.start(sent, sent_out))
    wait_all(puts)


def face_buffers(all_faces, factors):
    shapes = [pltpu.VMEM(all_faces.shape, f32), pltpu.VMEM(factors.shape, f32)]
    return shapes + [on_faces(), on_faces(), on_faces()]


def radiate(step, group, slots, reads, all_faces, factors, emissive, under, s):
    scratch = face_buffers(all_faces, factors)
    scratch += [on_faces(), pltpu.VMEM((group, TILES, TILE), f32)]
    outs = (ON_FACES, jax.ShapeDtypeStruct((group, TILES, TILE), f32))
    ins = (slots, reads, all_faces, factors, emissive, under, s)
    return call(functools.partial(faces_body, step), "faces_step", ins, outs, scratch, 10, 2)


def products(vectors):
    return [vectors[a] * vectors[b] for b in range(ITERS + 1) for a in range(b + 1)]


PAIRS = (ITERS + 1) * (ITERS + 2) // 2


def last_body(*refs):
    (slots, reads, u_in, base_in, all_in, factors_in, emissive_in, under_in, s_in) = refs[:9]
    (u0_in, u1_in, s0_in, s1_in) = refs[9:13]
    halos = refs[13:19]
    sent_out = refs[19]
    (u, base, u0, u1, all_faces, factors, emissive, under, s, s0, s1) = refs[20:31]
    (halo_y, halo_z, sent, sems) = refs[31:]
    copies = Copies(sems)
    get_u = in_chunks(copies, u_in, u, CY)
    gets = get_halos(copies, halos, u, halo_y, halo_z)
    fields = zip(*(in_chunks(copies, a, b) for a, b in ((base_in, base), (u0_in, u0), (u1_in, u1))))
    pairs = ((all_in, all_faces), (emissive_in, emissive), (under_in, under), (s_in, s))
    pairs += ((s0_in, s0), (s1_in, s1))
    small = [copies.start(a, b) for a, b in pairs]
    get_factors = in_chunks(copies, factors_in, factors)
    wait_all(get_u + gets)

    def new_block(i, made, sums):
        for q, (cur, new) in enumerate(made):
            at = pl.ds(pl.multiple_of(i * TILE + q * CY, CY), CY)
            terms = products([u0[at, :], u1[at, :], cur, new])
            sums = tuple(
                acc + ((p[0:8] + p[8:16]) + (p[16:24] + p[24:32])) for acc, p in zip(sums, terms)
            )
        return sums

    def new_faces(at, mine, new, sums):
        terms = products([s0[at, :], s1[at, :], mine, new])
        return tuple(acc + p for acc, p in zip(sums, terms))

    by_cells = tuple(jnp.zeros((8, CZ), f32) for _ in range(PAIRS))
    for c, parts in enumerate(fields):
        wait_all(parts)
        by_cells = stencil(ITERS - 1, c, u, base, halo_y, halo_z, new_block, by_cells)
    wait_all(small)
    by_faces = tuple(jnp.zeros((1, TILE), f32) for _ in range(PAIRS))
    for c in range(CHUNKS):
        get_factors[c].wait()
        by_faces = emission(
            ITERS - 1, c, slots, reads, factors, all_faces, emissive, s, under, new_faces, by_faces
        )
    spot = iota((1, CZ), 1)
    row = jnp.zeros((1, CZ), f32)
    for d in range(PAIRS):
        both = jnp.sum(by_cells[d], axis=0, keepdims=True) + by_faces[d]
        row = jnp.where(spot == d, jnp.sum(both, axis=1, keepdims=True), row)
    for q in range(sent.shape[0] // 8):
        sent[q * 8 : (q + 1) * 8, :] = jnp.broadcast_to(row, (8, CZ))
    copies.start(sent, sent_out).wait()


def last(devices, slots, reads, u, base, all_faces, factors, emissive, under, s, u0, u1, s0, s1, halos):
    scratch = [pltpu.VMEM((ROWS + 2 * CY, CZ), f32), field(), field(), field()]
    scratch += face_buffers(all_faces, factors) + [on_faces(), on_faces()]
    scratch += edge_buffers() + [pltpu.VMEM((devices, CZ), f32)]
    ins = (slots, reads, u, base, all_faces, factors, emissive, under, s, u0, u1, s0, s1, *halos)
    outs = (jax.ShapeDtypeStruct((devices, CZ), f32),)
    return call(last_body, "apply_and_reduce", ins, outs, scratch, 33, 2)[0]


def finish_body(*refs):
    (parts_in, u0_in, u1_in, u2_in, s0_in, s1_in, s2_in, out_u, out_s) = refs[:9]
    (parts, u0, u1, u2, s0, s1, s2, sems) = refs[9:]
    copies = Copies(sems)
    get_parts = copies.start(parts_in, parts)
    get_s = [copies.start(a, b) for a, b in ((s0_in, s0), (s1_in, s1), (s2_in, s2))]
    get_u = list(zip(*(in_chunks(copies, a, b) for a, b in ((u0_in, u0), (u1_in, u1), (u2_in, u2)))))
    get_parts.wait()
    total = jnp.sum(parts[...], axis=0, keepdims=True)
    entry = [total[:, d : d + 1] for d in range(10)]
    (g00, g01, g11, g02, g12, g22, g03, g13, g23, g33) = entry
    gram = [
        [g00, g01, g02, g03],
        [g01, g11, g12, g13],
        [g02, g12, g22, g23],
        [g03, g13, g23, g33],
    ]
    grow = 1.0 / SCALE
    image = [
        [SHIFTS[j] * gram[j][b] + grow * gram[j + 1][b] for b in range(ITERS + 1)]
        for j in range(ITERS)
    ]
    normal = [
        [SHIFTS[b] * image[a][b] + grow * image[a][b + 1] for b in range(ITERS)]
        for a in range(ITERS)
    ]
    target = [image[a][0] for a in range(ITERS)]
    for col in range(ITERS):
        for row in range(col + 1, ITERS):
            factor = normal[row][col] / normal[col][col]
            normal[row] = [normal[row][b] - factor * normal[col][b] for b in range(ITERS)]
            target[row] = target[row] - factor * target[col]
    coeffs = [None] * ITERS
    for row in range(ITERS - 1, -1, -1):
        acc = target[row]
        for b in range(row + 1, ITERS):
            acc = acc - normal[row][b] * coeffs[b]
        coeffs[row] = acc / normal[row][row]
    wide = [jnp.broadcast_to(c, (8, TILE)) for c in coeffs]

    def mix(ref, others):
        def rows(i, carry):
            at = pl.ds(pl.multiple_of(i * 8, 8), 8)
            ref[at, :] = (
                wide[0] * ref[at, :] + wide[1] * others[0][at, :] + wide[2] * others[1][at, :]
            )
            return carry

        return rows

    wait_all(get_s)
    lax.fori_loop(0, TILES // 8, mix(s0, (s1, s2)), 0, unroll=2)
    puts = [copies.start(s0, out_s)]
    for c, gets in enumerate(get_u):
        wait_all(gets)
        lax.fori_loop(c * PART // 8, (c + 1) * PART // 8, mix(u0, (u1, u2)), 0, unroll=8)
        at = pl.ds(c * PART, PART)
        puts.append(copies.start(u0.at[at], out_u.at[at]))
    wait_all(puts)


def finish(parts, fields, faces):
    scratch = [pltpu.VMEM(parts.shape, f32)] + [field()] * 3 + [on_faces()] * 3
    return call(finish_body, "finish", (parts, *fields, *faces), (FIELD, ON_FACES), scratch, 21)


def exchanged(sides):
    halos = []
    for axis, pair in zip(AXES, (sides[0:2], sides[2:4], sides[4:6])):
        size = lax.axis_size(axis)
        even = [(i, i ^ 1) for i in range(size)]
        odd = [(i, i + 1) for i in range(1, size - 1, 2)]
        odd += [(b, a) for a, b in odd]
        halos += [lax.ppermute(pair[0], axis, even), lax.ppermute(pair[1], axis, odd)]
    return halos


def local(
    rhs_cells, heat_diag, rhs_faces, emissive, view_factors, tile_slots, read_lists, face_cells
):
    slab = ("gy", "gz")
    group = lax.axis_size(slab)
    devices = lax.axis_size(AXES)
    slots = tile_slots.T
    reads = read_lists[0].T
    flat = (ROWS, CZ)
    fields, faces = [rhs_cells.reshape(flat)], [rhs_faces]
    sent = jnp.broadcast_to(rhs_faces[None], (group,) + rhs_faces.shape)
    heat = heat_diag.reshape(flat)
    for j in range(ITERS):
        u, s = fields[j], faces[j]
        all_faces = lax.all_to_all(sent, slab, 0, 0, tiled=True).reshape(-1, TILE)
        if j == 0:
            base, under, *sides = first(u, s, face_cells, heat)
            halos = exchanged(sides)
        if j + 1 < ITERS:
            s, sent = radiate(
                j, group, slots, reads, all_faces, view_factors, emissive, under, s
            )
            sent, halos = lax.optimization_barrier((sent, halos))
            u, base, under, *sides = cells(j, u, base, s, face_cells, heat, halos)
            halos = exchanged(sides)
            fields.append(u)
            faces.append(s)
        else:
            dots = last(
                devices, slots, reads, u, base, all_faces, view_factors, emissive, under, s,
                *fields[:j], *faces[:j], halos,
            )
    sums = lax.all_to_all(dots[:, None, :], AXES, 0, 0, tiled=True)
    sol_cells, sol_faces = finish(sums.reshape(devices, CZ), fields, faces)
    return (sol_cells.reshape(CX, CY, CZ), sol_faces)


def solution(mesh):
    placed = (
        P("gx", "gy", "gz"),
        P("gx", "gy", "gz"),
        P(("gx", "gy", "gz"), None),
        P(("gx", "gy", "gz"), None),
        P(("gx", "gy", "gz"), None, None, None),
        P(("gx", "gy", "gz"), None),
        P(("gx", "gy", "gz"), None, None),
        P(("gx", "gy", "gz"), None),
    )
    return jax.shard_map(
        local,
        mesh=mesh,
        in_specs=placed,
        out_specs=(P("gx", "gy", "gz"), P(("gx", "gy", "gz"), None)),
        check_vma=False,
    )
```

```python
import functools

import jax
import jax.numpy as jnp
from jax import lax
from jax.experimental import pallas as pl
from jax.experimental.pallas import tpu as pltpu
from jax.sharding import PartitionSpec as P

ITERS = 3
SHIFTS = (6.0, 3.0, 11.0)
SCALE = 0.125
CX, CY, CZ = 64, 32, 128
ROWS = CX * CY
TILES = 16
TILE = 128
FACES = TILES * TILE
SLOTS = 4
PER_OWNER = 4
f32 = jnp.float32
bf16 = jnp.bfloat16
VMEM = pl.BlockSpec(memory_space=pltpu.VMEM)
SMEM = pl.BlockSpec(memory_space=pltpu.SMEM)
HBM = pl.BlockSpec(memory_space=pltpu.HBM)
AXES = ("gx", "gy", "gz")
FIELD = jax.ShapeDtypeStruct((ROWS, CZ), f32)
ON_FACES = jax.ShapeDtypeStruct((TILES, TILE), f32)
CHUNKS = 4
PART = ROWS // CHUNKS
SIDE = ((CY, CZ), (CX, CZ), (TILES, TILE))
SIDES = tuple(jax.ShapeDtypeStruct(shape, f32) for shape in SIDE for _ in range(2))


def params(mib):
    return pltpu.CompilerParams(vmem_limit_bytes=mib << 20)


def split(x):
    high = x.astype(bf16)
    return high, (x - high.astype(f32)).astype(bf16)


def iota(shape, dim):
    return lax.broadcasted_iota(jnp.int32, shape, dim)


class Copies:
    def __init__(self, sems):
        self.sems = sems
        self.used = 0

    def start(self, source, target):
        copy = pltpu.make_async_copy(source, target, self.sems.at[self.used])
        self.used += 1
        copy.start()
        return copy


def outward(axis):
    odd = lax.rem(lax.axis_index(axis), 2)
    return 1 - odd, odd


def send_sides(copies, cells, edge_y, edge_z, sides):
    started = []
    for side, out in zip(outward("gx"), sides[0:2]):
        started.append(copies.start(cells.at[pl.ds(side * (ROWS - CY), CY), :], out))
    for edge, axis, outs in ((edge_y, "gy", sides[2:4]), (edge_z, "gz", sides[4:6])):
        for side, out in zip(outward(axis), outs):
            started.append(copies.start(edge.at[side], out))
    return started


def beside_z(group_z):
    z = lax.axis_index("gz")
    return z, lax.axis_index("gy") * group_z + z


def mark(rows, place):
    number = iota((ROWS, TILE), 0).astype(jnp.int16)
    one = jnp.ones((ROWS, TILE), bf16)
    zero = jnp.zeros((ROWS, TILE), bf16)

    def tile(i, carry):
        row = lax.shift_right_logical(place[pl.ds(i, 1), :], 7)
        row = jnp.broadcast_to(row, (16, TILE)).astype(jnp.int16)
        row = jnp.concatenate([row] * (ROWS // 16), axis=0)
        at = pl.ds(pl.multiple_of(i * TILE, TILE), TILE)
        rows[:, at] = jnp.where(number == row, one, zero)
        return carry

    lax.fori_loop(0, TILES, tile, 0)


def turn(u, wide, edge_z=None):
    def tile(i, carry):
        at = pl.ds(pl.multiple_of(i * TILE, TILE), TILE)
        part = u[at, :].T
        if edge_z is not None:
            edge_z[0, pl.ds(i, 1), :] = part[0:1, :]
            edge_z[1, pl.ds(i, 1), :] = part[CZ - 1 : CZ, :]
        high, low = split(part)
        wide[0:CZ, at] = high
        wide[CZ : 2 * CZ, at] = low
        return carry

    lax.fori_loop(0, TILES, tile, 0, unroll=4)


def look(rows, place, wide, under):
    z = iota((CZ, TILE), 0)
    width = TILES // CHUNKS
    for c in range(CHUNKS):
        at = slice(c * width * TILE, (c + 1) * width * TILE)
        seen = jnp.dot(wide[...], rows[:, at], preferred_element_type=f32)
        both = seen[0:CZ] + seen[CZ : 2 * CZ]
        for h in range(width):
            i = c * width + h
            here = z == (place[i : i + 1, :] & (CZ - 1))
            part = jnp.where(here, both[:, h * TILE : (h + 1) * TILE], 0.0)
            under[i : i + 1, :] = jnp.sum(part, axis=0, keepdims=True)


def lay(s, under, place, spread):
    z = iota((CZ, TILE), 0)

    def tile(i, carry):
        at = pl.ds(pl.multiple_of(i * TILE, TILE), TILE)
        here = z == (place[pl.ds(i, 1), :] & (CZ - 1))
        high, low = split(1.0 * (under[pl.ds(i, 1), :] - s[pl.ds(i, 1), :]))
        spread[0:CZ, at] = jnp.where(here, high.astype(f32), 0.0).astype(bf16)
        spread[CZ : 2 * CZ, at] = jnp.where(here, low.astype(f32), 0.0).astype(bf16)
        return carry

    lax.fori_loop(0, TILES, tile, 0, unroll=4)


def meet(copies, shift, u, s, rows, place, heat, spread, wide, under, base_out, under_out):
    look(rows, place, wide, under)
    puts = [copies.start(under, under_out)]
    lay(s, under, place, spread)
    for c in range(CHUNKS):
        at = pl.ds(c * PART, PART)
        sums = lax.dot_general(
            rows[at, :], spread[...], (((1,), (1,)), ((), ())), preferred_element_type=f32
        )
        heat[at, :] = (heat[at, :] + (6.0 - shift)) * u[at, :] + (
            sums[:, 0:CZ] + sums[:, CZ : 2 * CZ]
        )
        puts.append(copies.start(heat.at[at], base_out.at[at]))
    return puts


def wait_all(copies):
    for copy in copies:
        copy.wait()


def first_body(*refs):
    (u_in, s_in, place_in, heat_in, base_out, under_out) = refs[:6]
    sides = refs[6:12]
    (u, s, place, heat, rows, under, edge_y, edge_z, spread, wide, sems) = refs[12:]
    copies = Copies(sems)
    get_place = copies.start(place_in, place)
    get_u = copies.start(u_in, u)
    rest = [copies.start(s_in, s), copies.start(heat_in, heat)]
    get_place.wait()
    mark(rows, place)
    get_u.wait()
    for x in range(CX):
        edge_y[0, x : x + 1, :] = u[x * CY : x * CY + 1, :]
        edge_y[1, x : x + 1, :] = u[(x + 1) * CY - 1 : (x + 1) * CY, :]
    turn(u, wide, edge_z)
    puts = send_sides(copies, u, edge_y, edge_z, sides)
    wait_all(rest)
    puts += meet(
        copies, SHIFTS[0], u, s, rows, place, heat, spread, wide, under, base_out, under_out
    )
    wait_all(puts)


def field():
    return pltpu.VMEM((ROWS, CZ), f32)


def on_faces(dtype=f32):
    return pltpu.VMEM((TILES, TILE), dtype)


def one_hot():
    return pltpu.VMEM((ROWS, FACES), bf16)


def edge_buffers():
    return [pltpu.VMEM((2, CX, CZ), f32), pltpu.VMEM((2, TILES, TILE), f32)]


def call(body, name, ins, outs, scratch, sems, smem=0):
    specs = [SMEM] * smem + [HBM] * (len(ins) - smem)
    return pl.pallas_call(
        body,
        out_shape=tuple(outs),
        in_specs=specs,
        out_specs=(HBM,) * len(outs),
        scratch_shapes=list(scratch) + [pltpu.SemaphoreType.DMA((sems,))],
        compiler_params=params(64),
        name=name,
    )(*ins)


def parts():
    return [pltpu.VMEM((2 * CZ, FACES), bf16), pltpu.VMEM((2 * CZ, FACES), bf16)]


def first(u, s, place, heat):
    scratch = [field(), on_faces(), on_faces(jnp.int32), field(), one_hot(), on_faces()]
    scratch += edge_buffers() + parts()
    return call(
        first_body, "first_meet", (u, s, place, heat), (FIELD, ON_FACES) + SIDES, scratch, 15
    )


def stencil(step, chunk, u, base, edge_y, edge_z, new_block, sums):
    sub = iota((CY, CZ), 0)
    lane = iota((CY, CZ), 1)
    z = iota((CZ, TILE), 0)

    def block(i, sums):
        at_z = pl.ds(i, 1)
        facing = jnp.where(z == 0, edge_z[0, at_z, :], 0.0)
        facing = jnp.where(z == CZ - 1, edge_z[1, at_z, :], facing).T
        made = []
        for q in range(4):
            x = i * 4 + q
            row = pl.multiple_of(x * CY, CY)
            cur = u[pl.ds(row + CY, CY), :]
            beside = u[pl.ds(row, CY), :] + u[pl.ds(row + 2 * CY, CY), :]
            at_y = pl.ds(x, 1)
            low = jnp.where(sub == 0, edge_y[0, at_y, :], pltpu.roll(cur, 1, 0))
            high = jnp.where(sub == CY - 1, edge_y[1, at_y, :], pltpu.roll(cur, CY - 1, 0))
            beside = beside + (low + high)
            low = jnp.where(lane == 0, 0.0, pltpu.roll(cur, 1, 1))
            high = jnp.where(lane == CZ - 1, 0.0, pltpu.roll(cur, CZ - 1, 1))
            beside = beside + (low + high) + facing[q * CY : (q + 1) * CY, :]
            made.append((cur, (base[pl.ds(row, CY), :] - beside) * SCALE))
        return new_block(i, made, sums)

    count = TILES // CHUNKS
    return lax.fori_loop(chunk * count, (chunk + 1) * count, block, sums, unroll=2)


def emission(step, chunk, per_owner, slots, reads, factors, all_faces, emissive, own, under, new_faces, sums):
    eye = iota((TILE, TILE), 0) == iota((TILE, TILE), 1)

    def tile(i, sums):
        acc = None
        for k in range(SLOTS):
            slot = slots[k, i]
            owner = lax.shift_right_logical(slot, 2)
            column = owner * per_owner + reads[slot & (PER_OWNER - 1), owner]
            term = factors[i, k] * all_faces[pl.ds(column, 1), :]
            acc = term if acc is None else acc + term
        row = jnp.sum(acc, axis=1, keepdims=True)
        flux = jnp.sum(jnp.where(eye, row, 0.0), axis=0, keepdims=True)
        at = pl.ds(i, 1)
        mine = own[at, :]
        e = emissive[at, :]
        new = ((1.0 - SHIFTS[step] + e) * mine - under[at, :] - e * flux) * SCALE
        return new_faces(at, mine, new, sums)

    count = TILES // CHUNKS
    return lax.fori_loop(chunk * count, (chunk + 1) * count, tile, sums, unroll=count)


def get_halos(copies, group_z, halos, received, u, edge_y, edge_z):
    started = []
    for side, halo in zip(outward("gx"), halos[0:2]):
        started.append(copies.start(halo, u.at[pl.ds(side * (ROWS + CY), CY), :]))
    for edge, axis, pair in ((edge_y, "gy", halos[2:4]), (edge_z, "gz", halos[4:6])):
        for side, halo in zip(outward(axis), pair):
            started.append(copies.start(halo, edge.at[side]))
    if len(halos) == 4:
        z, mine = beside_z(group_z)
        for side, (there, peer) in enumerate(((z > 0, mine - 1), (z < group_z - 1, mine + 1))):
            row = jnp.where(there, peer, mine) * (2 * TILES) + TILES
            started.append(copies.start(received.at[pl.ds(row, TILES), :], edge_z.at[side]))
    return started


def clear_ends(group_z, halos, edge_z):
    if len(halos) == 4:
        z = lax.axis_index("gz")
        for side, there in enumerate((z > 0, z < group_z - 1)):
            edge_z[side] = jnp.where(there, edge_z[side], 0.0)


def in_chunks(copies, source, target, offset=0):
    part = source.shape[0] // CHUNKS
    return [
        copies.start(source.at[pl.ds(c * part, part)], target.at[pl.ds(offset + c * part, part)])
        for c in range(CHUNKS)
    ]


def middle_body(step, group_z, count, *refs):
    (slots, reads, u_in, base_in, all_in, factors_in, emissive_in, under_in, s_in) = refs[:9]
    (place_in, heat_in) = refs[9:11]
    halos, refs = refs[11 : 11 + count], refs[11 + count :]
    (u_out, s_out, sent_out, base_out, under_out) = refs[:5]
    sides = refs[5:9]
    (u, base, all_faces, factors, emissive, under, s, place, heat) = refs[9:18]
    (new_u, new_s, sent, halo_y, halo_z, edge_y, edge_z, rows, spread, wide, sems) = refs[18:]
    copies = Copies(sems)
    get_place = copies.start(place_in, place)
    get_u = in_chunks(copies, u_in, u, CY)
    gets = get_halos(copies, group_z, halos, all_in, u, halo_y, halo_z)
    get_base = in_chunks(copies, base_in, base)
    pairs = ((all_in, all_faces), (emissive_in, emissive), (under_in, under), (s_in, s))
    get_faces = [copies.start(a, b) for a, b in pairs]
    get_factors = in_chunks(copies, factors_in, factors)
    get_heat = copies.start(heat_in, heat)
    get_place.wait()
    mark(rows, place)
    wait_all(get_u + gets)
    clear_ends(group_z, halos, halo_z)

    def new_block(i, made, sums):
        for q, (_, new) in enumerate(made):
            new_u[pl.ds(pl.multiple_of(i * TILE + q * CY, CY), CY), :] = new
            edge_y[0, pl.ds(i * 4 + q, 1), :] = new[0:1, :]
            edge_y[1, pl.ds(i * 4 + q, 1), :] = new[CY - 1 : CY, :]
        return sums

    def new_faces(at, mine, new, sums):
        new_s[at, :] = new
        return sums

    puts = []
    for c in range(CHUNKS):
        get_base[c].wait()
        stencil(step, c, u, base, halo_y, halo_z, new_block, 0)
        at = pl.ds(c * PART, PART)
        puts.append(copies.start(new_u.at[at], u_out.at[at]))
    turn(new_u, wide, edge_z)
    puts += send_sides(copies, new_u, edge_y, edge_z, sides)
    wait_all(get_faces)
    per_owner = all_faces.shape[0] // sent.shape[0]
    for c in range(CHUNKS):
        get_factors[c].wait()
        emission(
            step, c, per_owner, slots, reads, factors, all_faces, emissive, s, under, new_faces, 0
        )
    puts.append(copies.start(new_s, s_out))
    z, mine = beside_z(group_z)
    value = new_s[...]
    low = edge_z[0]
    high = edge_z[1]
    for q in range(sent.shape[0]):
        sent[q, 0:TILES] = value
        sent[q, TILES : 2 * TILES] = jnp.where(mine - 1 == q, low, high)
    puts.append(copies.start(sent, sent_out))
    get_heat.wait()
    puts += meet(
        copies, SHIFTS[step + 1], new_u, new_s, rows, place, heat, spread, wide, under,
        base_out, under_out,
    )
    wait_all(puts)


def middle(
    step, group, group_z, slots, reads, u, base, all_faces, factors, emissive, under, s, place, heat,
    halos,
):
    scratch = [pltpu.VMEM((ROWS + 2 * CY, CZ), f32), field()] + face_buffers(all_faces, factors)
    scratch += [on_faces(jnp.int32), field(), field(), on_faces()]
    scratch += [pltpu.VMEM((group, 2 * TILES, TILE), f32)]
    scratch += edge_buffers() + edge_buffers() + [one_hot()] + parts()
    body = functools.partial(middle_body, step, group_z, len(halos))
    outs = (FIELD, ON_FACES, jax.ShapeDtypeStruct((group, 2 * TILES, TILE), f32), FIELD, ON_FACES)
    ins = (slots, reads, u, base, all_faces, factors, emissive, under, s, place, heat, *halos)
    return call(body, "apply_and_meet", ins, outs + SIDES[:4], scratch, 40, 2)


def face_buffers(all_faces, factors):
    shapes = [pltpu.VMEM(all_faces.shape, f32), pltpu.VMEM(factors.shape, f32)]
    return shapes + [on_faces(), on_faces(), on_faces()]


def products(vectors):
    return [vectors[a] * vectors[b] for b in range(ITERS + 1) for a in range(b + 1)]


PAIRS = (ITERS + 1) * (ITERS + 2) // 2


def last_body(group_z, *refs):
    (slots, reads, u_in, base_in, all_in, factors_in, emissive_in, under_in, s_in) = refs[:9]
    (u0_in, u1_in, s0_in, s1_in) = refs[9:13]
    halos = refs[13:17]
    sent_out = refs[17]
    (u, base, u0, u1, all_faces, factors, emissive, under, s, s0, s1) = refs[18:29]
    (halo_y, halo_z, sent, sems) = refs[29:]
    copies = Copies(sems)
    get_u = in_chunks(copies, u_in, u, CY)
    gets = get_halos(copies, group_z, halos, all_in, u, halo_y, halo_z)
    fields = zip(*(in_chunks(copies, a, b) for a, b in ((base_in, base), (u0_in, u0), (u1_in, u1))))
    pairs = ((all_in, all_faces), (emissive_in, emissive), (under_in, under), (s_in, s))
    pairs += ((s0_in, s0), (s1_in, s1))
    small = [copies.start(a, b) for a, b in pairs]
    get_factors = in_chunks(copies, factors_in, factors)
    wait_all(get_u + gets)
    clear_ends(group_z, halos, halo_z)

    def new_block(i, made, sums):
        for q, (cur, new) in enumerate(made):
            at = pl.ds(pl.multiple_of(i * TILE + q * CY, CY), CY)
            terms = products([u0[at, :], u1[at, :], cur, new])
            sums = tuple(
                acc + ((p[0:8] + p[8:16]) + (p[16:24] + p[24:32])) for acc, p in zip(sums, terms)
            )
        return sums

    def new_faces(at, mine, new, sums):
        terms = products([s0[at, :], s1[at, :], mine, new])
        return tuple(acc + p for acc, p in zip(sums, terms))

    by_cells = tuple(jnp.zeros((8, CZ), f32) for _ in range(PAIRS))
    for c, parts in enumerate(fields):
        wait_all(parts)
        by_cells = stencil(ITERS - 1, c, u, base, halo_y, halo_z, new_block, by_cells)
    wait_all(small)
    by_faces = tuple(jnp.zeros((1, TILE), f32) for _ in range(PAIRS))
    for c in range(CHUNKS):
        get_factors[c].wait()
        by_faces = emission(
            ITERS - 1, c, 2 * TILES, slots, reads, factors, all_faces, emissive, s, under, new_faces,
            by_faces,
        )
    spot = iota((1, CZ), 1)
    row = jnp.zeros((1, CZ), f32)
    for d in range(PAIRS):
        both = jnp.sum(by_cells[d], axis=0, keepdims=True) + by_faces[d]
        row = jnp.where(spot == d, jnp.sum(both, axis=1, keepdims=True), row)
    for q in range(sent.shape[0] // 8):
        sent[q * 8 : (q + 1) * 8, :] = jnp.broadcast_to(row, (8, CZ))
    copies.start(sent, sent_out).wait()


def last(devices, group_z, slots, reads, u, base, all_faces, factors, emissive, under, s, u0, u1, s0, s1, halos):
    scratch = [pltpu.VMEM((ROWS + 2 * CY, CZ), f32), field(), field(), field()]
    scratch += face_buffers(all_faces, factors) + [on_faces(), on_faces()]
    scratch += edge_buffers() + [pltpu.VMEM((devices, CZ), f32)]
    ins = (slots, reads, u, base, all_faces, factors, emissive, under, s, u0, u1, s0, s1, *halos)
    outs = (jax.ShapeDtypeStruct((devices, CZ), f32),)
    return call(functools.partial(last_body, group_z), "apply_and_reduce", ins, outs, scratch, 33, 2)[0]


def finish_body(*refs):
    (parts_in, u0_in, u1_in, u2_in, s0_in, s1_in, s2_in, out_u, out_s) = refs[:9]
    (parts, u0, u1, u2, s0, s1, s2, sems) = refs[9:]
    copies = Copies(sems)
    get_parts = copies.start(parts_in, parts)
    get_s = [copies.start(a, b) for a, b in ((s0_in, s0), (s1_in, s1), (s2_in, s2))]
    get_u = list(zip(*(in_chunks(copies, a, b) for a, b in ((u0_in, u0), (u1_in, u1), (u2_in, u2)))))
    get_parts.wait()
    total = jnp.sum(parts[...], axis=0, keepdims=True)
    entry = [total[:, d : d + 1] for d in range(10)]
    (g00, g01, g11, g02, g12, g22, g03, g13, g23, g33) = entry
    gram = [
        [g00, g01, g02, g03],
        [g01, g11, g12, g13],
        [g02, g12, g22, g23],
        [g03, g13, g23, g33],
    ]
    grow = 1.0 / SCALE
    image = [
        [SHIFTS[j] * gram[j][b] + grow * gram[j + 1][b] for b in range(ITERS + 1)]
        for j in range(ITERS)
    ]
    normal = [
        [SHIFTS[b] * image[a][b] + grow * image[a][b + 1] for b in range(ITERS)]
        for a in range(ITERS)
    ]
    target = [image[a][0] for a in range(ITERS)]
    for col in range(ITERS):
        for row in range(col + 1, ITERS):
            factor = normal[row][col] / normal[col][col]
            normal[row] = [normal[row][b] - factor * normal[col][b] for b in range(ITERS)]
            target[row] = target[row] - factor * target[col]
    coeffs = [None] * ITERS
    for row in range(ITERS - 1, -1, -1):
        acc = target[row]
        for b in range(row + 1, ITERS):
            acc = acc - normal[row][b] * coeffs[b]
        coeffs[row] = acc / normal[row][row]
    wide = [jnp.broadcast_to(c, (8, TILE)) for c in coeffs]

    def mix(ref, others):
        def rows(i, carry):
            at = pl.ds(pl.multiple_of(i * 8, 8), 8)
            ref[at, :] = (
                wide[0] * ref[at, :] + wide[1] * others[0][at, :] + wide[2] * others[1][at, :]
            )
            return carry

        return rows

    wait_all(get_s)
    lax.fori_loop(0, TILES // 8, mix(s0, (s1, s2)), 0, unroll=2)
    puts = [copies.start(s0, out_s)]
    for c, gets in enumerate(get_u):
        wait_all(gets)
        lax.fori_loop(c * PART // 8, (c + 1) * PART // 8, mix(u0, (u1, u2)), 0, unroll=8)
        at = pl.ds(c * PART, PART)
        puts.append(copies.start(u0.at[at], out_u.at[at]))
    wait_all(puts)


def finish(parts, fields, faces):
    scratch = [pltpu.VMEM(parts.shape, f32)] + [field()] * 3 + [on_faces()] * 3
    return call(finish_body, "finish", (parts, *fields, *faces), (FIELD, ON_FACES), scratch, 21)


def exchanged(sides):
    halos = []
    for axis, pair in zip(AXES, [sides[n : n + 2] for n in range(0, len(sides), 2)]):
        size = lax.axis_size(axis)
        even = [(i, i ^ 1) for i in range(size)]
        odd = [(i, i + 1) for i in range(1, size - 1, 2)]
        odd += [(b, a) for a, b in odd]
        halos += [lax.ppermute(pair[0], axis, even), lax.ppermute(pair[1], axis, odd)]
    return halos


def local(
    rhs_cells, heat_diag, rhs_faces, emissive, view_factors, tile_slots, read_lists, face_cells
):
    slab = ("gy", "gz")
    group = lax.axis_size(slab)
    group_z = lax.axis_size("gz")
    devices = lax.axis_size(AXES)
    slots = tile_slots.T
    reads = read_lists[0].T
    flat = (ROWS, CZ)
    fields, faces = [rhs_cells.reshape(flat)], [rhs_faces]
    sent = jnp.broadcast_to(rhs_faces[None], (group,) + rhs_faces.shape)
    heat = heat_diag.reshape(flat)
    for j in range(ITERS):
        u, s = fields[j], faces[j]
        all_faces = lax.all_to_all(sent, slab, 0, 0, tiled=True).reshape(-1, TILE)
        if j == 0:
            base, under, *sides = first(u, s, face_cells, heat)
            halos = exchanged(sides)
        given = (slots, reads, u, base, all_faces, view_factors, emissive, under, s)
        if j + 1 < ITERS:
            u, s, sent, base, under, *sides = middle(
                j, group, group_z, *given, face_cells, heat, halos
            )
            halos = exchanged(sides)
            fields.append(u)
            faces.append(s)
        else:
            dots = last(devices, group_z, *given, *fields[:j], *faces[:j], halos)
    sums = lax.all_to_all(dots[:, None, :], AXES, 0, 0, tiled=True)
    sol_cells, sol_faces = finish(sums.reshape(devices, CZ), fields, faces)
    return (sol_cells.reshape(CX, CY, CZ), sol_faces)


def solution(mesh):
    placed = (
        P("gx", "gy", "gz"),
        P("gx", "gy", "gz"),
        P(("gx", "gy", "gz"), None),
        P(("gx", "gy", "gz"), None),
        P(("gx", "gy", "gz"), None, None, None),
        P(("gx", "gy", "gz"), None),
        P(("gx", "gy", "gz"), None, None),
        P(("gx", "gy", "gz"), None),
    )
    return jax.shard_map(
        local,
        mesh=mesh,
        in_specs=placed,
        out_specs=(P("gx", "gy", "gz"), P(("gx", "gy", "gz"), None)),
        check_vma=False,
    )
```

```python
import functools

import jax
import jax.numpy as jnp
from jax import lax
from jax.experimental import pallas as pl
from jax.experimental.pallas import tpu as pltpu
from jax.sharding import PartitionSpec as P

ITERS = 3
SHIFTS = (6.0, 3.0, 11.0)
SCALE = 0.125
CX, CY, CZ = 64, 32, 128
ROWS = CX * CY
TILES = 16
TILE = 128
FACES = TILES * TILE
SLOTS = 4
PER_OWNER = 4
f32 = jnp.float32
bf16 = jnp.bfloat16
VMEM = pl.BlockSpec(memory_space=pltpu.VMEM)
SMEM = pl.BlockSpec(memory_space=pltpu.SMEM)
HBM = pl.BlockSpec(memory_space=pltpu.HBM)
AXES = ("gx", "gy", "gz")
FIELD = jax.ShapeDtypeStruct((ROWS, CZ), f32)
ON_FACES = jax.ShapeDtypeStruct((TILES, TILE), f32)
CHUNKS = 4
PART = ROWS // CHUNKS
SIDE = ((CY, CZ), (CX, CZ), (TILES, TILE))
SIDES = tuple(jax.ShapeDtypeStruct(shape, f32) for shape in SIDE for _ in range(2))


def params(mib):
    return pltpu.CompilerParams(vmem_limit_bytes=mib << 20)


def split(x):
    high = x.astype(bf16)
    return high, (x - high.astype(f32)).astype(bf16)


def iota(shape, dim):
    return lax.broadcasted_iota(jnp.int32, shape, dim)


class Copies:
    def __init__(self, sems):
        self.sems = sems
        self.used = 0

    def start(self, source, target):
        copy = pltpu.make_async_copy(source, target, self.sems.at[self.used])
        self.used += 1
        copy.start()
        return copy


def outward(axis):
    odd = lax.rem(lax.axis_index(axis), 2)
    return 1 - odd, odd


def send_sides(copies, cells, edge_y, edge_z, sides):
    started = []
    for side, out in zip(outward("gx"), sides[0:2]):
        started.append(copies.start(cells.at[pl.ds(side * (ROWS - CY), CY), :], out))
    for edge, axis, outs in ((edge_y, "gy", sides[2:4]), (edge_z, "gz", sides[4:6])):
        for side, out in zip(outward(axis), outs):
            started.append(copies.start(edge.at[side], out))
    return started


def beside_z(group_z):
    z = lax.axis_index("gz")
    return z, lax.axis_index("gy") * group_z + z


def mark(rows, place):
    number = iota((ROWS, TILE), 0).astype(jnp.int16)
    one = jnp.ones((ROWS, TILE), bf16)
    zero = jnp.zeros((ROWS, TILE), bf16)

    def tile(i, carry):
        row = lax.shift_right_logical(place[pl.ds(i, 1), :], 7)
        row = jnp.broadcast_to(row, (16, TILE)).astype(jnp.int16)
        row = jnp.concatenate([row] * (ROWS // 16), axis=0)
        at = pl.ds(pl.multiple_of(i * TILE, TILE), TILE)
        rows[:, at] = jnp.where(number == row, one, zero)
        return carry

    lax.fori_loop(0, TILES, tile, 0)


def turn(u, wide, edge_z=None):
    def tile(i, carry):
        at = pl.ds(pl.multiple_of(i * TILE, TILE), TILE)
        part = u[at, :].T
        if edge_z is not None:
            edge_z[0, pl.ds(i, 1), :] = part[0:1, :]
            edge_z[1, pl.ds(i, 1), :] = part[CZ - 1 : CZ, :]
        high, low = split(part)
        wide[0:CZ, at] = high
        wide[CZ : 2 * CZ, at] = low
        return carry

    lax.fori_loop(0, TILES, tile, 0, unroll=4)


def look(rows, place, wide, under, beside=None):
    z = iota((CZ, TILE), 0)
    width = TILES // CHUNKS
    for c in range(CHUNKS):
        at = slice(c * width * TILE, (c + 1) * width * TILE)
        if beside is not None:
            beside(c)
        seen = jnp.dot(wide[...], rows[:, at], preferred_element_type=f32)
        both = seen[0:CZ] + seen[CZ : 2 * CZ]
        for h in range(width):
            i = c * width + h
            here = z == (place[i : i + 1, :] & (CZ - 1))
            part = jnp.where(here, both[:, h * TILE : (h + 1) * TILE], 0.0)
            under[i : i + 1, :] = jnp.sum(part, axis=0, keepdims=True)


def lay(s, under, place, spread):
    z = iota((CZ, TILE), 0)

    def tile(i, carry):
        at = pl.ds(pl.multiple_of(i * TILE, TILE), TILE)
        here = z == (place[pl.ds(i, 1), :] & (CZ - 1))
        high, low = split(1.0 * (under[pl.ds(i, 1), :] - s[pl.ds(i, 1), :]))
        spread[0:CZ, at] = jnp.where(here, high.astype(f32), 0.0).astype(bf16)
        spread[CZ : 2 * CZ, at] = jnp.where(here, low.astype(f32), 0.0).astype(bf16)
        return carry

    lax.fori_loop(0, TILES, tile, 0, unroll=4)


def meet(copies, shift, u, s, rows, place, heat, spread, under, base_out, under_out):
    puts = [copies.start(under, under_out)]
    lay(s, under, place, spread)
    for c in range(CHUNKS):
        at = pl.ds(c * PART, PART)
        sums = lax.dot_general(
            rows[at, :], spread[...], (((1,), (1,)), ((), ())), preferred_element_type=f32
        )
        heat[at, :] = (heat[at, :] + (6.0 - shift)) * u[at, :] + (
            sums[:, 0:CZ] + sums[:, CZ : 2 * CZ]
        )
        puts.append(copies.start(heat.at[at], base_out.at[at]))
    return puts


def wait_all(copies):
    for copy in copies:
        copy.wait()


def first_body(*refs):
    (u_in, s_in, place_in, heat_in, base_out, under_out) = refs[:6]
    sides = refs[6:12]
    (u, s, place, heat, rows, under, edge_y, edge_z, spread, wide, sems) = refs[12:]
    copies = Copies(sems)
    get_place = copies.start(place_in, place)
    get_u = copies.start(u_in, u)
    rest = [copies.start(s_in, s), copies.start(heat_in, heat)]
    get_place.wait()
    mark(rows, place)
    get_u.wait()
    for x in range(CX):
        edge_y[0, x : x + 1, :] = u[x * CY : x * CY + 1, :]
        edge_y[1, x : x + 1, :] = u[(x + 1) * CY - 1 : (x + 1) * CY, :]
    turn(u, wide, edge_z)
    puts = send_sides(copies, u, edge_y, edge_z, sides)
    wait_all(rest)
    look(rows, place, wide, under)
    puts += meet(copies, SHIFTS[0], u, s, rows, place, heat, spread, under, base_out, under_out)
    wait_all(puts)


def field():
    return pltpu.VMEM((ROWS, CZ), f32)


def on_faces(dtype=f32):
    return pltpu.VMEM((TILES, TILE), dtype)


def one_hot():
    return pltpu.VMEM((ROWS, FACES), bf16)


def edge_buffers():
    return [pltpu.VMEM((2, CX, CZ), f32), pltpu.VMEM((2, TILES, TILE), f32)]


def call(body, name, ins, outs, scratch, sems, smem=0):
    specs = [SMEM] * smem + [HBM] * (len(ins) - smem)
    return pl.pallas_call(
        body,
        out_shape=tuple(outs),
        in_specs=specs,
        out_specs=(HBM,) * len(outs),
        scratch_shapes=list(scratch) + [pltpu.SemaphoreType.DMA((sems,))],
        compiler_params=params(64),
        name=name,
    )(*ins)


def parts():
    return [pltpu.VMEM((2 * CZ, FACES), bf16), pltpu.VMEM((2 * CZ, FACES), bf16)]


def first(u, s, place, heat):
    scratch = [field(), on_faces(), on_faces(jnp.int32), field(), one_hot(), on_faces()]
    scratch += edge_buffers() + parts()
    return call(
        first_body, "first_meet", (u, s, place, heat), (FIELD, ON_FACES) + SIDES, scratch, 15
    )


def stencil(step, chunk, u, base, edge_y, edge_z, new_block, sums):
    sub = iota((CY, CZ), 0)
    lane = iota((CY, CZ), 1)
    z = iota((CZ, TILE), 0)

    def block(i, sums):
        at_z = pl.ds(i, 1)
        facing = jnp.where(z == 0, edge_z[0, at_z, :], 0.0)
        facing = jnp.where(z == CZ - 1, edge_z[1, at_z, :], facing).T
        made = []
        for q in range(4):
            x = i * 4 + q
            row = pl.multiple_of(x * CY, CY)
            cur = u[pl.ds(row + CY, CY), :]
            beside = u[pl.ds(row, CY), :] + u[pl.ds(row + 2 * CY, CY), :]
            at_y = pl.ds(x, 1)
            low = jnp.where(sub == 0, edge_y[0, at_y, :], pltpu.roll(cur, 1, 0))
            high = jnp.where(sub == CY - 1, edge_y[1, at_y, :], pltpu.roll(cur, CY - 1, 0))
            beside = beside + (low + high)
            low = jnp.where(lane == 0, 0.0, pltpu.roll(cur, 1, 1))
            high = jnp.where(lane == CZ - 1, 0.0, pltpu.roll(cur, CZ - 1, 1))
            beside = beside + (low + high) + facing[q * CY : (q + 1) * CY, :]
            made.append((cur, (base[pl.ds(row, CY), :] - beside) * SCALE))
        return new_block(i, made, sums)

    count = TILES // CHUNKS
    return lax.fori_loop(chunk * count, (chunk + 1) * count, block, sums, unroll=2)


def emission(step, chunk, per_owner, slots, reads, factors, all_faces, emissive, own, under, new_faces, sums):
    eye = iota((TILE, TILE), 0) == iota((TILE, TILE), 1)

    def tile(i, sums):
        acc = None
        for k in range(SLOTS):
            slot = slots[k, i]
            owner = lax.shift_right_logical(slot, 2)
            column = owner * per_owner + reads[slot & (PER_OWNER - 1), owner]
            term = factors[i, k] * all_faces[pl.ds(column, 1), :]
            acc = term if acc is None else acc + term
        row = jnp.sum(acc, axis=1, keepdims=True)
        flux = jnp.sum(jnp.where(eye, row, 0.0), axis=0, keepdims=True)
        at = pl.ds(i, 1)
        mine = own[at, :]
        e = emissive[at, :]
        new = ((1.0 - SHIFTS[step] + e) * mine - under[at, :] - e * flux) * SCALE
        return new_faces(at, mine, new, sums)

    count = TILES // CHUNKS
    return lax.fori_loop(chunk * count, (chunk + 1) * count, tile, sums, unroll=count)


def get_halos(copies, group_z, halos, received, u, edge_y, edge_z):
    started = []
    for side, halo in zip(outward("gx"), halos[0:2]):
        started.append(copies.start(halo, u.at[pl.ds(side * (ROWS + CY), CY), :]))
    for edge, axis, pair in ((edge_y, "gy", halos[2:4]), (edge_z, "gz", halos[4:6])):
        for side, halo in zip(outward(axis), pair):
            started.append(copies.start(halo, edge.at[side]))
    if len(halos) == 4:
        z, mine = beside_z(group_z)
        for side, (there, peer) in enumerate(((z > 0, mine - 1), (z < group_z - 1, mine + 1))):
            row = jnp.where(there, peer, mine) * (2 * TILES) + TILES
            started.append(copies.start(received.at[pl.ds(row, TILES), :], edge_z.at[side]))
    return started


def clear_ends(group_z, halos, edge_z):
    if len(halos) == 4:
        z = lax.axis_index("gz")
        for side, there in enumerate((z > 0, z < group_z - 1)):
            edge_z[side] = jnp.where(there, edge_z[side], 0.0)


def in_chunks(copies, source, target, offset=0):
    part = source.shape[0] // CHUNKS
    return [
        copies.start(source.at[pl.ds(c * part, part)], target.at[pl.ds(offset + c * part, part)])
        for c in range(CHUNKS)
    ]


def middle_body(step, group_z, count, *refs):
    (slots, reads, u_in, base_in, all_in, factors_in, emissive_in, under_in, s_in) = refs[:9]
    (place_in, heat_in) = refs[9:11]
    halos, refs = refs[11 : 11 + count], refs[11 + count :]
    (u_out, s_out, sent_out, base_out, under_out) = refs[:5]
    sides = refs[5:9]
    (u, base, all_faces, factors, emissive, under, s, place, heat) = refs[9:18]
    (new_u, new_s, new_under, sent, halo_y, halo_z, edge_y, edge_z) = refs[18:26]
    (rows, spread, wide, sems) = refs[26:]
    copies = Copies(sems)
    get_place = copies.start(place_in, place)
    get_u = in_chunks(copies, u_in, u, CY)
    gets = get_halos(copies, group_z, halos, all_in, u, halo_y, halo_z)
    get_base = in_chunks(copies, base_in, base)
    pairs = ((all_in, all_faces), (emissive_in, emissive), (under_in, under), (s_in, s))
    get_faces = [copies.start(a, b) for a, b in pairs]
    get_factors = in_chunks(copies, factors_in, factors)
    get_heat = copies.start(heat_in, heat)
    get_place.wait()
    mark(rows, place)
    wait_all(get_u + gets)
    clear_ends(group_z, halos, halo_z)

    def new_block(i, made, sums):
        for q, (_, new) in enumerate(made):
            new_u[pl.ds(pl.multiple_of(i * TILE + q * CY, CY), CY), :] = new
            edge_y[0, pl.ds(i * 4 + q, 1), :] = new[0:1, :]
            edge_y[1, pl.ds(i * 4 + q, 1), :] = new[CY - 1 : CY, :]
        return sums

    def new_faces(at, mine, new, sums):
        new_s[at, :] = new
        return sums

    puts = []
    for c in range(CHUNKS):
        get_base[c].wait()
        stencil(step, c, u, base, halo_y, halo_z, new_block, 0)
        at = pl.ds(c * PART, PART)
        puts.append(copies.start(new_u.at[at], u_out.at[at]))
    turn(new_u, wide, edge_z)
    puts += send_sides(copies, new_u, edge_y, edge_z, sides)
    wait_all(get_faces + get_factors)
    per_owner = all_faces.shape[0] // sent.shape[0]

    def radiate(c):
        emission(
            step, c, per_owner, slots, reads, factors, all_faces, emissive, s, under, new_faces, 0
        )

    look(rows, place, wide, new_under, radiate)
    puts.append(copies.start(new_s, s_out))
    z, mine = beside_z(group_z)
    value = new_s[...]
    low = edge_z[0]
    high = edge_z[1]
    for q in range(sent.shape[0]):
        sent[q, 0:TILES] = value
        sent[q, TILES : 2 * TILES] = jnp.where(mine - 1 == q, low, high)
    puts.append(copies.start(sent, sent_out))
    get_heat.wait()
    puts += meet(
        copies, SHIFTS[step + 1], new_u, new_s, rows, place, heat, spread, new_under,
        base_out, under_out,
    )
    wait_all(puts)


def middle(
    step, group, group_z, slots, reads, u, base, all_faces, factors, emissive, under, s, place, heat,
    halos,
):
    scratch = [pltpu.VMEM((ROWS + 2 * CY, CZ), f32), field()] + face_buffers(all_faces, factors)
    scratch += [on_faces(jnp.int32), field(), field(), on_faces(), on_faces()]
    scratch += [pltpu.VMEM((group, 2 * TILES, TILE), f32)]
    scratch += edge_buffers() + edge_buffers() + [one_hot()] + parts()
    body = functools.partial(middle_body, step, group_z, len(halos))
    outs = (FIELD, ON_FACES, jax.ShapeDtypeStruct((group, 2 * TILES, TILE), f32), FIELD, ON_FACES)
    ins = (slots, reads, u, base, all_faces, factors, emissive, under, s, place, heat, *halos)
    return call(body, "apply_and_meet", ins, outs + SIDES[:4], scratch, 40, 2)


def face_buffers(all_faces, factors):
    shapes = [pltpu.VMEM(all_faces.shape, f32), pltpu.VMEM(factors.shape, f32)]
    return shapes + [on_faces(), on_faces(), on_faces()]


def products(vectors):
    return [vectors[a] * vectors[b] for b in range(ITERS + 1) for a in range(b + 1)]


PAIRS = (ITERS + 1) * (ITERS + 2) // 2


def last_body(group_z, *refs):
    (slots, reads, u_in, base_in, all_in, factors_in, emissive_in, under_in, s_in) = refs[:9]
    (u0_in, u1_in, s0_in, s1_in) = refs[9:13]
    halos = refs[13:17]
    sent_out = refs[17]
    (u, base, u0, u1, all_faces, factors, emissive, under, s, s0, s1) = refs[18:29]
    (halo_y, halo_z, sent, sems) = refs[29:]
    copies = Copies(sems)
    get_u = in_chunks(copies, u_in, u, CY)
    gets = get_halos(copies, group_z, halos, all_in, u, halo_y, halo_z)
    fields = []
    for c in range(CHUNKS):
        at = pl.ds(c * PART, PART)
        pairs = ((base_in, base), (u0_in, u0), (u1_in, u1))
        fields.append([copies.start(a.at[at], b.at[at]) for a, b in pairs])
    pairs = ((all_in, all_faces), (emissive_in, emissive), (under_in, under), (s_in, s))
    pairs += ((s0_in, s0), (s1_in, s1))
    small = [copies.start(a, b) for a, b in pairs]
    get_factors = in_chunks(copies, factors_in, factors)
    wait_all(get_u + gets)
    clear_ends(group_z, halos, halo_z)

    def new_block(i, made, sums):
        for q, (cur, new) in enumerate(made):
            at = pl.ds(pl.multiple_of(i * TILE + q * CY, CY), CY)
            terms = products([u0[at, :], u1[at, :], cur, new])
            sums = tuple(
                acc + ((p[0:8] + p[8:16]) + (p[16:24] + p[24:32])) for acc, p in zip(sums, terms)
            )
        return sums

    def new_faces(at, mine, new, sums):
        terms = products([s0[at, :], s1[at, :], mine, new])
        return tuple(acc + p for acc, p in zip(sums, terms))

    by_cells = tuple(jnp.zeros((8, CZ), f32) for _ in range(PAIRS))
    for c, parts in enumerate(fields):
        wait_all(parts)
        by_cells = stencil(ITERS - 1, c, u, base, halo_y, halo_z, new_block, by_cells)
    wait_all(small)
    by_faces = tuple(jnp.zeros((1, TILE), f32) for _ in range(PAIRS))
    for c in range(CHUNKS):
        get_factors[c].wait()
        by_faces = emission(
            ITERS - 1, c, 2 * TILES, slots, reads, factors, all_faces, emissive, s, under, new_faces,
            by_faces,
        )
    spot = iota((1, CZ), 1)
    row = jnp.zeros((1, CZ), f32)
    for d in range(PAIRS):
        both = jnp.sum(by_cells[d], axis=0, keepdims=True) + by_faces[d]
        row = jnp.where(spot == d, jnp.sum(both, axis=1, keepdims=True), row)
    for q in range(sent.shape[0] // 8):
        sent[q * 8 : (q + 1) * 8, :] = jnp.broadcast_to(row, (8, CZ))
    copies.start(sent, sent_out).wait()


def last(devices, group_z, slots, reads, u, base, all_faces, factors, emissive, under, s, u0, u1, s0, s1, halos):
    scratch = [pltpu.VMEM((ROWS + 2 * CY, CZ), f32), field(), field(), field()]
    scratch += face_buffers(all_faces, factors) + [on_faces(), on_faces()]
    scratch += edge_buffers() + [pltpu.VMEM((devices, CZ), f32)]
    ins = (slots, reads, u, base, all_faces, factors, emissive, under, s, u0, u1, s0, s1, *halos)
    outs = (jax.ShapeDtypeStruct((devices, CZ), f32),)
    return call(functools.partial(last_body, group_z), "apply_and_reduce", ins, outs, scratch, 33, 2)[0]


def finish_body(*refs):
    (parts_in, u0_in, u1_in, u2_in, s0_in, s1_in, s2_in, out_u, out_s) = refs[:9]
    (parts, u0, u1, u2, s0, s1, s2, sems) = refs[9:]
    copies = Copies(sems)
    get_parts = copies.start(parts_in, parts)
    get_s = [copies.start(a, b) for a, b in ((s0_in, s0), (s1_in, s1), (s2_in, s2))]
    get_u = list(zip(*(in_chunks(copies, a, b) for a, b in ((u0_in, u0), (u1_in, u1), (u2_in, u2)))))
    get_parts.wait()
    total = jnp.sum(parts[...], axis=0, keepdims=True)
    entry = [total[:, d : d + 1] for d in range(10)]
    (g00, g01, g11, g02, g12, g22, g03, g13, g23, g33) = entry
    gram = [
        [g00, g01, g02, g03],
        [g01, g11, g12, g13],
        [g02, g12, g22, g23],
        [g03, g13, g23, g33],
    ]
    grow = 1.0 / SCALE
    image = [
        [SHIFTS[j] * gram[j][b] + grow * gram[j + 1][b] for b in range(ITERS + 1)]
        for j in range(ITERS)
    ]
    normal = [
        [SHIFTS[b] * image[a][b] + grow * image[a][b + 1] for b in range(ITERS)]
        for a in range(ITERS)
    ]
    target = [image[a][0] for a in range(ITERS)]
    for col in range(ITERS):
        for row in range(col + 1, ITERS):
            factor = normal[row][col] / normal[col][col]
            normal[row] = [normal[row][b] - factor * normal[col][b] for b in range(ITERS)]
            target[row] = target[row] - factor * target[col]
    coeffs = [None] * ITERS
    for row in range(ITERS - 1, -1, -1):
        acc = target[row]
        for b in range(row + 1, ITERS):
            acc = acc - normal[row][b] * coeffs[b]
        coeffs[row] = acc / normal[row][row]
    wide = [jnp.broadcast_to(c, (8, TILE)) for c in coeffs]

    def mix(ref, others):
        def rows(i, carry):
            at = pl.ds(pl.multiple_of(i * 8, 8), 8)
            ref[at, :] = (
                wide[0] * ref[at, :] + wide[1] * others[0][at, :] + wide[2] * others[1][at, :]
            )
            return carry

        return rows

    wait_all(get_s)
    lax.fori_loop(0, TILES // 8, mix(s0, (s1, s2)), 0, unroll=2)
    puts = [copies.start(s0, out_s)]
    for c, gets in enumerate(get_u):
        wait_all(gets)
        lax.fori_loop(c * PART // 8, (c + 1) * PART // 8, mix(u0, (u1, u2)), 0, unroll=8)
        at = pl.ds(c * PART, PART)
        puts.append(copies.start(u0.at[at], out_u.at[at]))
    wait_all(puts)


def finish(parts, fields, faces):
    scratch = [pltpu.VMEM(parts.shape, f32)] + [field()] * 3 + [on_faces()] * 3
    return call(finish_body, "finish", (parts, *fields, *faces), (FIELD, ON_FACES), scratch, 21)


def exchanged(sides):
    halos = []
    for axis, pair in zip(AXES, [sides[n : n + 2] for n in range(0, len(sides), 2)]):
        size = lax.axis_size(axis)
        even = [(i, i ^ 1) for i in range(size)]
        odd = [(i, i + 1) for i in range(1, size - 1, 2)]
        odd += [(b, a) for a, b in odd]
        halos += [lax.ppermute(pair[0], axis, even), lax.ppermute(pair[1], axis, odd)]
    return halos


def local(
    rhs_cells, heat_diag, rhs_faces, emissive, view_factors, tile_slots, read_lists, face_cells
):
    slab = ("gy", "gz")
    group = lax.axis_size(slab)
    group_z = lax.axis_size("gz")
    devices = lax.axis_size(AXES)
    slots = tile_slots.T
    reads = read_lists[0].T
    flat = (ROWS, CZ)
    fields, faces = [rhs_cells.reshape(flat)], [rhs_faces]
    sent = jnp.broadcast_to(rhs_faces[None], (group,) + rhs_faces.shape)
    heat = heat_diag.reshape(flat)
    for j in range(ITERS):
        u, s = fields[j], faces[j]
        all_faces = lax.all_to_all(sent, slab, 0, 0, tiled=True).reshape(-1, TILE)
        if j == 0:
            base, under, *sides = first(u, s, face_cells, heat)
            halos = exchanged(sides)
        given = (slots, reads, u, base, all_faces, view_factors, emissive, under, s)
        if j + 1 < ITERS:
            u, s, sent, base, under, *sides = middle(
                j, group, group_z, *given, face_cells, heat, halos
            )
            halos = exchanged(sides)
            fields.append(u)
            faces.append(s)
        else:
            dots = last(devices, group_z, *given, *fields[:j], *faces[:j], halos)
    sums = lax.all_to_all(dots[:, None, :], AXES, 0, 0, tiled=True)
    sol_cells, sol_faces = finish(sums.reshape(devices, CZ), fields, faces)
    return (sol_cells.reshape(CX, CY, CZ), sol_faces)


def solution(mesh):
    placed = (
        P("gx", "gy", "gz"),
        P("gx", "gy", "gz"),
        P(("gx", "gy", "gz"), None),
        P(("gx", "gy", "gz"), None),
        P(("gx", "gy", "gz"), None, None, None),
        P(("gx", "gy", "gz"), None),
        P(("gx", "gy", "gz"), None, None),
        P(("gx", "gy", "gz"), None),
    )
    return jax.shard_map(
        local,
        mesh=mesh,
        in_specs=placed,
        out_specs=(P("gx", "gy", "gz"), P(("gx", "gy", "gz"), None)),
        check_vma=False,
    )
```

```python
import functools

import jax
import jax.numpy as jnp
from jax import lax
from jax.experimental import pallas as pl
from jax.experimental.pallas import tpu as pltpu
from jax.sharding import PartitionSpec as P

ITERS = 3
SHIFTS = (6.0, 3.0, 11.0)
SCALE = 0.125
CX, CY, CZ = 64, 32, 128
ROWS = CX * CY
TILES = 16
TILE = 128
FACES = TILES * TILE
SLOTS = 4
PER_OWNER = 4
f32 = jnp.float32
bf16 = jnp.bfloat16
VMEM = pl.BlockSpec(memory_space=pltpu.VMEM)
SMEM = pl.BlockSpec(memory_space=pltpu.SMEM)
HBM = pl.BlockSpec(memory_space=pltpu.HBM)
AXES = ("gx", "gy", "gz")
FIELD = jax.ShapeDtypeStruct((ROWS, CZ), f32)
ON_FACES = jax.ShapeDtypeStruct((TILES, TILE), f32)
CHUNKS = 4
PART = ROWS // CHUNKS
SIDE = ((CY, CZ), (CX, CZ), (TILES, TILE))
SIDES = tuple(jax.ShapeDtypeStruct(shape, f32) for shape in SIDE for _ in range(2))


def params(mib):
    return pltpu.CompilerParams(vmem_limit_bytes=mib << 20)


def split(x):
    high = x.astype(bf16)
    return high, (x - high.astype(f32)).astype(bf16)


def iota(shape, dim):
    return lax.broadcasted_iota(jnp.int32, shape, dim)


class Copies:
    def __init__(self, sems):
        self.sems = sems
        self.used = 0

    def start(self, source, target):
        copy = pltpu.make_async_copy(source, target, self.sems.at[self.used])
        self.used += 1
        copy.start()
        return copy


def outward(axis):
    odd = lax.rem(lax.axis_index(axis), 2)
    return 1 - odd, odd


def send_sides(copies, cells, edge_y, edge_z, sides):
    started = []
    for side, out in zip(outward("gx"), sides[0:2]):
        started.append(copies.start(cells.at[pl.ds(side * (ROWS - CY), CY), :], out))
    for edge, axis, outs in ((edge_y, "gy", sides[2:4]), (edge_z, "gz", sides[4:6])):
        for side, out in zip(outward(axis), outs):
            started.append(copies.start(edge.at[side], out))
    return started


def beside_z(group_z):
    z = lax.axis_index("gz")
    return z, lax.axis_index("gy") * group_z + z


def mark(rows, place):
    number = iota((ROWS, TILE), 0).astype(jnp.int16)
    one = jnp.ones((ROWS, TILE), bf16)
    zero = jnp.zeros((ROWS, TILE), bf16)

    def tile(i, carry):
        row = lax.shift_right_logical(place[pl.ds(i, 1), :], 7)
        row = jnp.broadcast_to(row, (16, TILE)).astype(jnp.int16)
        row = jnp.concatenate([row] * (ROWS // 16), axis=0)
        at = pl.ds(pl.multiple_of(i * TILE, TILE), TILE)
        rows[:, at] = jnp.where(number == row, one, zero)
        return carry

    lax.fori_loop(0, TILES, tile, 0)


def turn(u, wide, edge_z=None):
    def tile(i, carry):
        at = pl.ds(pl.multiple_of(i * TILE, TILE), TILE)
        part = u[at, :].T
        if edge_z is not None:
            edge_z[0, pl.ds(i, 1), :] = part[0:1, :]
            edge_z[1, pl.ds(i, 1), :] = part[CZ - 1 : CZ, :]
        high, low = split(part)
        wide[0:CZ, at] = high
        wide[CZ : 2 * CZ, at] = low
        return carry

    lax.fori_loop(0, TILES, tile, 0, unroll=4)


def look(rows, place, wide, under, beside=None):
    z = iota((CZ, TILE), 0)
    width = TILES // CHUNKS
    for c in range(CHUNKS):
        at = slice(c * width * TILE, (c + 1) * width * TILE)
        if beside is not None:
            beside(c)
        seen = jnp.dot(wide[...], rows[:, at], preferred_element_type=f32)
        both = seen[0:CZ] + seen[CZ : 2 * CZ]
        for h in range(width):
            i = c * width + h
            here = z == (place[i : i + 1, :] & (CZ - 1))
            part = jnp.where(here, both[:, h * TILE : (h + 1) * TILE], 0.0)
            under[i : i + 1, :] = jnp.sum(part, axis=0, keepdims=True)


def lay(s, under, place, spread):
    z = iota((CZ, TILE), 0)

    def tile(i, carry):
        at = pl.ds(pl.multiple_of(i * TILE, TILE), TILE)
        here = z == (place[pl.ds(i, 1), :] & (CZ - 1))
        high, low = split(1.0 * (under[pl.ds(i, 1), :] - s[pl.ds(i, 1), :]))
        spread[0:CZ, at] = jnp.where(here, high.astype(f32), 0.0).astype(bf16)
        spread[CZ : 2 * CZ, at] = jnp.where(here, low.astype(f32), 0.0).astype(bf16)
        return carry

    lax.fori_loop(0, TILES, tile, 0, unroll=4)


def meet(copies, shift, u, s, rows, place, heat, spread, under, base_out, under_out):
    puts = [copies.start(under, under_out)]
    lay(s, under, place, spread)
    for c in range(CHUNKS):
        at = pl.ds(c * PART, PART)
        sums = lax.dot_general(
            rows[at, :], spread[...], (((1,), (1,)), ((), ())), preferred_element_type=f32
        )
        heat[at, :] = (heat[at, :] + (6.0 - shift)) * u[at, :] + (
            sums[:, 0:CZ] + sums[:, CZ : 2 * CZ]
        )
        puts.append(copies.start(heat.at[at], base_out.at[at]))
    return puts


def wait_all(copies):
    for copy in copies:
        copy.wait()


def pack(group_z, sent, s, edge_z):
    z, mine = beside_z(group_z)
    value = s[...]
    low = edge_z[0]
    high = edge_z[1]
    for q in range(sent.shape[0]):
        sent[q, 0:TILES] = value
        sent[q, TILES : 2 * TILES] = jnp.where(mine - 1 == q, low, high)


def first_body(group_z, *refs):
    (u_in, s_in, place_in, heat_in, base_out, under_out, sent_out) = refs[:7]
    sides = refs[7:11]
    (u, s, place, heat, rows, under, sent, edge_y, edge_z, spread, wide, sems) = refs[11:]
    copies = Copies(sems)
    get_place = copies.start(place_in, place)
    get_u = copies.start(u_in, u)
    rest = [copies.start(s_in, s), copies.start(heat_in, heat)]
    get_place.wait()
    mark(rows, place)
    get_u.wait()
    for x in range(CX):
        edge_y[0, x : x + 1, :] = u[x * CY : x * CY + 1, :]
        edge_y[1, x : x + 1, :] = u[(x + 1) * CY - 1 : (x + 1) * CY, :]
    turn(u, wide, edge_z)
    puts = send_sides(copies, u, edge_y, edge_z, sides)
    wait_all(rest)
    pack(group_z, sent, s, edge_z)
    puts.append(copies.start(sent, sent_out))
    look(rows, place, wide, under)
    puts += meet(copies, SHIFTS[0], u, s, rows, place, heat, spread, under, base_out, under_out)
    wait_all(puts)


def field():
    return pltpu.VMEM((ROWS, CZ), f32)


def on_faces(dtype=f32):
    return pltpu.VMEM((TILES, TILE), dtype)


def one_hot():
    return pltpu.VMEM((ROWS, FACES), bf16)


def edge_buffers():
    return [pltpu.VMEM((2, CX, CZ), f32), pltpu.VMEM((2, TILES, TILE), f32)]


def call(body, name, ins, outs, scratch, sems, smem=0):
    specs = [SMEM] * smem + [HBM] * (len(ins) - smem)
    return pl.pallas_call(
        body,
        out_shape=tuple(outs),
        in_specs=specs,
        out_specs=(HBM,) * len(outs),
        scratch_shapes=list(scratch) + [pltpu.SemaphoreType.DMA((sems,))],
        compiler_params=params(64),
        name=name,
    )(*ins)


def parts():
    return [pltpu.VMEM((2 * CZ, FACES), bf16), pltpu.VMEM((2 * CZ, FACES), bf16)]


def first(group, group_z, u, s, place, heat):
    scratch = [field(), on_faces(), on_faces(jnp.int32), field(), one_hot(), on_faces()]
    scratch += [pltpu.VMEM((group, 2 * TILES, TILE), f32)] + edge_buffers() + parts()
    outs = (FIELD, ON_FACES, jax.ShapeDtypeStruct((group, 2 * TILES, TILE), f32)) + SIDES[:4]
    body = functools.partial(first_body, group_z)
    return call(body, "first_meet", (u, s, place, heat), outs, scratch, 15)


def stencil(step, chunk, u, base, edge_y, edge_z, new_block, sums):
    sub = iota((CY, CZ), 0)
    lane = iota((CY, CZ), 1)
    z = iota((CZ, TILE), 0)

    def block(i, sums):
        at_z = pl.ds(i, 1)
        facing = jnp.where(z == 0, edge_z[0, at_z, :], 0.0)
        facing = jnp.where(z == CZ - 1, edge_z[1, at_z, :], facing).T
        made = []
        for q in range(4):
            x = i * 4 + q
            row = pl.multiple_of(x * CY, CY)
            cur = u[pl.ds(row + CY, CY), :]
            beside = u[pl.ds(row, CY), :] + u[pl.ds(row + 2 * CY, CY), :]
            at_y = pl.ds(x, 1)
            low = jnp.where(sub == 0, edge_y[0, at_y, :], pltpu.roll(cur, 1, 0))
            high = jnp.where(sub == CY - 1, edge_y[1, at_y, :], pltpu.roll(cur, CY - 1, 0))
            beside = beside + (low + high)
            low = jnp.where(lane == 0, 0.0, pltpu.roll(cur, 1, 1))
            high = jnp.where(lane == CZ - 1, 0.0, pltpu.roll(cur, CZ - 1, 1))
            beside = beside + (low + high) + facing[q * CY : (q + 1) * CY, :]
            made.append((cur, (base[pl.ds(row, CY), :] - beside) * SCALE))
        return new_block(i, made, sums)

    count = TILES // CHUNKS
    return lax.fori_loop(chunk * count, (chunk + 1) * count, block, sums, unroll=2)


def emission(step, chunk, per_owner, slots, reads, factors, all_faces, emissive, own, under, new_faces, sums):
    eye = iota((TILE, TILE), 0) == iota((TILE, TILE), 1)

    def tile(i, sums):
        acc = None
        for k in range(SLOTS):
            slot = slots[k, i]
            owner = lax.shift_right_logical(slot, 2)
            column = owner * per_owner + reads[slot & (PER_OWNER - 1), owner]
            term = factors[i, k] * all_faces[pl.ds(column, 1), :]
            acc = term if acc is None else acc + term
        row = jnp.sum(acc, axis=1, keepdims=True)
        flux = jnp.sum(jnp.where(eye, row, 0.0), axis=0, keepdims=True)
        at = pl.ds(i, 1)
        mine = own[at, :]
        e = emissive[at, :]
        new = ((1.0 - SHIFTS[step] + e) * mine - under[at, :] - e * flux) * SCALE
        return new_faces(at, mine, new, sums)

    count = TILES // CHUNKS
    return lax.fori_loop(chunk * count, (chunk + 1) * count, tile, sums, unroll=count)


def get_halos(copies, group_z, halos, received, u, edge_y, edge_z):
    started = []
    for side, halo in zip(outward("gx"), halos[0:2]):
        started.append(copies.start(halo, u.at[pl.ds(side * (ROWS + CY), CY), :]))
    for edge, axis, pair in ((edge_y, "gy", halos[2:4]), (edge_z, "gz", halos[4:6])):
        for side, halo in zip(outward(axis), pair):
            started.append(copies.start(halo, edge.at[side]))
    if len(halos) == 4:
        z, mine = beside_z(group_z)
        for side, (there, peer) in enumerate(((z > 0, mine - 1), (z < group_z - 1, mine + 1))):
            row = jnp.where(there, peer, mine) * (2 * TILES) + TILES
            started.append(copies.start(received.at[pl.ds(row, TILES), :], edge_z.at[side]))
    return started


def clear_ends(group_z, halos, edge_z):
    if len(halos) == 4:
        z = lax.axis_index("gz")
        for side, there in enumerate((z > 0, z < group_z - 1)):
            edge_z[side] = jnp.where(there, edge_z[side], 0.0)


def in_chunks(copies, source, target, offset=0):
    part = source.shape[0] // CHUNKS
    return [
        copies.start(source.at[pl.ds(c * part, part)], target.at[pl.ds(offset + c * part, part)])
        for c in range(CHUNKS)
    ]


def middle_body(step, group_z, count, *refs):
    (slots, reads, u_in, base_in, all_in, factors_in, emissive_in, under_in, s_in) = refs[:9]
    (place_in, heat_in) = refs[9:11]
    halos, refs = refs[11 : 11 + count], refs[11 + count :]
    (u_out, s_out, sent_out, base_out, under_out) = refs[:5]
    sides = refs[5:9]
    (u, base, all_faces, factors, emissive, under, s, place, heat) = refs[9:18]
    (new_u, new_s, new_under, sent, halo_y, halo_z, edge_y, edge_z) = refs[18:26]
    (rows, spread, wide, sems) = refs[26:]
    copies = Copies(sems)
    get_place = copies.start(place_in, place)
    get_u = in_chunks(copies, u_in, u, CY)
    gets = get_halos(copies, group_z, halos, all_in, u, halo_y, halo_z)
    get_base = in_chunks(copies, base_in, base)
    pairs = ((all_in, all_faces), (emissive_in, emissive), (under_in, under), (s_in, s))
    get_faces = [copies.start(a, b) for a, b in pairs]
    get_factors = in_chunks(copies, factors_in, factors)
    get_heat = copies.start(heat_in, heat)
    get_place.wait()
    mark(rows, place)
    wait_all(get_u + gets)
    clear_ends(group_z, halos, halo_z)

    def new_block(i, made, sums):
        for q, (_, new) in enumerate(made):
            new_u[pl.ds(pl.multiple_of(i * TILE + q * CY, CY), CY), :] = new
            edge_y[0, pl.ds(i * 4 + q, 1), :] = new[0:1, :]
            edge_y[1, pl.ds(i * 4 + q, 1), :] = new[CY - 1 : CY, :]
        return sums

    def new_faces(at, mine, new, sums):
        new_s[at, :] = new
        return sums

    puts = []
    for c in range(CHUNKS):
        get_base[c].wait()
        stencil(step, c, u, base, halo_y, halo_z, new_block, 0)
        at = pl.ds(c * PART, PART)
        puts.append(copies.start(new_u.at[at], u_out.at[at]))
    turn(new_u, wide, edge_z)
    puts += send_sides(copies, new_u, edge_y, edge_z, sides)
    wait_all(get_faces + get_factors)
    per_owner = all_faces.shape[0] // sent.shape[0]

    def radiate(c):
        emission(
            step, c, per_owner, slots, reads, factors, all_faces, emissive, s, under, new_faces, 0
        )

    look(rows, place, wide, new_under, radiate)
    puts.append(copies.start(new_s, s_out))
    pack(group_z, sent, new_s, edge_z)
    puts.append(copies.start(sent, sent_out))
    get_heat.wait()
    puts += meet(
        copies, SHIFTS[step + 1], new_u, new_s, rows, place, heat, spread, new_under,
        base_out, under_out,
    )
    wait_all(puts)


def middle(
    step, group, group_z, slots, reads, u, base, all_faces, factors, emissive, under, s, place, heat,
    halos,
):
    scratch = [pltpu.VMEM((ROWS + 2 * CY, CZ), f32), field()] + face_buffers(all_faces, factors)
    scratch += [on_faces(jnp.int32), field(), field(), on_faces(), on_faces()]
    scratch += [pltpu.VMEM((group, 2 * TILES, TILE), f32)]
    scratch += edge_buffers() + edge_buffers() + [one_hot()] + parts()
    body = functools.partial(middle_body, step, group_z, len(halos))
    outs = (FIELD, ON_FACES, jax.ShapeDtypeStruct((group, 2 * TILES, TILE), f32), FIELD, ON_FACES)
    ins = (slots, reads, u, base, all_faces, factors, emissive, under, s, place, heat, *halos)
    return call(body, "apply_and_meet", ins, outs + SIDES[:4], scratch, 40, 2)


def face_buffers(all_faces, factors):
    shapes = [pltpu.VMEM(all_faces.shape, f32), pltpu.VMEM(factors.shape, f32)]
    return shapes + [on_faces(), on_faces(), on_faces()]


def products(vectors):
    return [vectors[a] * vectors[b] for b in range(ITERS + 1) for a in range(b + 1)]


PAIRS = (ITERS + 1) * (ITERS + 2) // 2


def last_body(group_z, *refs):
    (slots, reads, u_in, base_in, all_in, factors_in, emissive_in, under_in, s_in) = refs[:9]
    (u0_in, u1_in, s0_in, s1_in) = refs[9:13]
    halos = refs[13:17]
    sent_out = refs[17]
    (u, base, u0, u1, all_faces, factors, emissive, under, s, s0, s1) = refs[18:29]
    (halo_y, halo_z, sent, sems) = refs[29:]
    copies = Copies(sems)
    get_u = in_chunks(copies, u_in, u, CY)
    gets = get_halos(copies, group_z, halos, all_in, u, halo_y, halo_z)
    fields = []
    for c in range(CHUNKS):
        at = pl.ds(c * PART, PART)
        pairs = ((base_in, base), (u0_in, u0), (u1_in, u1))
        fields.append([copies.start(a.at[at], b.at[at]) for a, b in pairs])
    pairs = ((all_in, all_faces), (emissive_in, emissive), (under_in, under), (s_in, s))
    pairs += ((s0_in, s0), (s1_in, s1))
    small = [copies.start(a, b) for a, b in pairs]
    get_factors = in_chunks(copies, factors_in, factors)
    wait_all(get_u + gets)
    clear_ends(group_z, halos, halo_z)

    def new_block(i, made, sums):
        for q, (cur, new) in enumerate(made):
            at = pl.ds(pl.multiple_of(i * TILE + q * CY, CY), CY)
            terms = products([u0[at, :], u1[at, :], cur, new])
            sums = tuple(
                acc + ((p[0:8] + p[8:16]) + (p[16:24] + p[24:32])) for acc, p in zip(sums, terms)
            )
        return sums

    def new_faces(at, mine, new, sums):
        terms = products([s0[at, :], s1[at, :], mine, new])
        return tuple(acc + p for acc, p in zip(sums, terms))

    by_cells = tuple(jnp.zeros((8, CZ), f32) for _ in range(PAIRS))
    for c, parts in enumerate(fields):
        wait_all(parts)
        by_cells = stencil(ITERS - 1, c, u, base, halo_y, halo_z, new_block, by_cells)
    wait_all(small)
    by_faces = tuple(jnp.zeros((1, TILE), f32) for _ in range(PAIRS))
    for c in range(CHUNKS):
        get_factors[c].wait()
        by_faces = emission(
            ITERS - 1, c, 2 * TILES, slots, reads, factors, all_faces, emissive, s, under, new_faces,
            by_faces,
        )
    spot = iota((1, CZ), 1)
    row = jnp.zeros((1, CZ), f32)
    for d in range(PAIRS):
        both = jnp.sum(by_cells[d], axis=0, keepdims=True) + by_faces[d]
        row = jnp.where(spot == d, jnp.sum(both, axis=1, keepdims=True), row)
    for q in range(sent.shape[0] // 8):
        sent[q * 8 : (q + 1) * 8, :] = jnp.broadcast_to(row, (8, CZ))
    copies.start(sent, sent_out).wait()


def last(devices, group_z, slots, reads, u, base, all_faces, factors, emissive, under, s, u0, u1, s0, s1, halos):
    scratch = [pltpu.VMEM((ROWS + 2 * CY, CZ), f32), field(), field(), field()]
    scratch += face_buffers(all_faces, factors) + [on_faces(), on_faces()]
    scratch += edge_buffers() + [pltpu.VMEM((devices, CZ), f32)]
    ins = (slots, reads, u, base, all_faces, factors, emissive, under, s, u0, u1, s0, s1, *halos)
    outs = (jax.ShapeDtypeStruct((devices, CZ), f32),)
    return call(functools.partial(last_body, group_z), "apply_and_reduce", ins, outs, scratch, 33, 2)[0]


def finish_body(*refs):
    (parts_in, u0_in, u1_in, u2_in, s0_in, s1_in, s2_in, out_u, out_s) = refs[:9]
    (parts, u0, u1, u2, s0, s1, s2, sems) = refs[9:]
    copies = Copies(sems)
    get_parts = copies.start(parts_in, parts)
    get_s = [copies.start(a, b) for a, b in ((s0_in, s0), (s1_in, s1), (s2_in, s2))]
    get_u = list(zip(*(in_chunks(copies, a, b) for a, b in ((u0_in, u0), (u1_in, u1), (u2_in, u2)))))
    get_parts.wait()
    total = jnp.sum(parts[...], axis=0, keepdims=True)
    entry = [total[:, d : d + 1] for d in range(10)]
    (g00, g01, g11, g02, g12, g22, g03, g13, g23, g33) = entry
    gram = [
        [g00, g01, g02, g03],
        [g01, g11, g12, g13],
        [g02, g12, g22, g23],
        [g03, g13, g23, g33],
    ]
    grow = 1.0 / SCALE
    image = [
        [SHIFTS[j] * gram[j][b] + grow * gram[j + 1][b] for b in range(ITERS + 1)]
        for j in range(ITERS)
    ]
    normal = [
        [SHIFTS[b] * image[a][b] + grow * image[a][b + 1] for b in range(ITERS)]
        for a in range(ITERS)
    ]
    target = [image[a][0] for a in range(ITERS)]
    for col in range(ITERS):
        for row in range(col + 1, ITERS):
            factor = normal[row][col] / normal[col][col]
            normal[row] = [normal[row][b] - factor * normal[col][b] for b in range(ITERS)]
            target[row] = target[row] - factor * target[col]
    coeffs = [None] * ITERS
    for row in range(ITERS - 1, -1, -1):
        acc = target[row]
        for b in range(row + 1, ITERS):
            acc = acc - normal[row][b] * coeffs[b]
        coeffs[row] = acc / normal[row][row]
    wide = [jnp.broadcast_to(c, (8, TILE)) for c in coeffs]

    def mix(ref, others):
        def rows(i, carry):
            at = pl.ds(pl.multiple_of(i * 8, 8), 8)
            ref[at, :] = (
                wide[0] * ref[at, :] + wide[1] * others[0][at, :] + wide[2] * others[1][at, :]
            )
            return carry

        return rows

    wait_all(get_s)
    lax.fori_loop(0, TILES // 8, mix(s0, (s1, s2)), 0, unroll=2)
    puts = [copies.start(s0, out_s)]
    for c, gets in enumerate(get_u):
        wait_all(gets)
        lax.fori_loop(c * PART // 8, (c + 1) * PART // 8, mix(u0, (u1, u2)), 0, unroll=8)
        at = pl.ds(c * PART, PART)
        puts.append(copies.start(u0.at[at], out_u.at[at]))
    wait_all(puts)


def finish(parts, fields, faces):
    scratch = [pltpu.VMEM(parts.shape, f32)] + [field()] * 3 + [on_faces()] * 3
    return call(finish_body, "finish", (parts, *fields, *faces), (FIELD, ON_FACES), scratch, 21)


def exchanged(sides):
    halos = []
    for axis, pair in zip(AXES, [sides[n : n + 2] for n in range(0, len(sides), 2)]):
        size = lax.axis_size(axis)
        even = [(i, i ^ 1) for i in range(size)]
        odd = [(i, i + 1) for i in range(1, size - 1, 2)]
        odd += [(b, a) for a, b in odd]
        halos += [lax.ppermute(pair[0], axis, even), lax.ppermute(pair[1], axis, odd)]
    return halos


def local(
    rhs_cells, heat_diag, rhs_faces, emissive, view_factors, tile_slots, read_lists, face_cells
):
    slab = ("gy", "gz")
    group = lax.axis_size(slab)
    group_z = lax.axis_size("gz")
    devices = lax.axis_size(AXES)
    slots = tile_slots.T
    reads = read_lists[0].T
    flat = (ROWS, CZ)
    fields, faces = [rhs_cells.reshape(flat)], [rhs_faces]
    heat = heat_diag.reshape(flat)
    for j in range(ITERS):
        u, s = fields[j], faces[j]
        if j == 0:
            base, under, sent, *sides = first(group, group_z, u, s, face_cells, heat)
            halos = exchanged(sides)
        all_faces = lax.all_to_all(sent, slab, 0, 0, tiled=True).reshape(-1, TILE)
        given = (slots, reads, u, base, all_faces, view_factors, emissive, under, s)
        if j + 1 < ITERS:
            u, s, sent, base, under, *sides = middle(
                j, group, group_z, *given, face_cells, heat, halos
            )
            halos = exchanged(sides)
            fields.append(u)
            faces.append(s)
        else:
            dots = last(devices, group_z, *given, *fields[:j], *faces[:j], halos)
    sums = lax.all_to_all(dots[:, None, :], AXES, 0, 0, tiled=True)
    sol_cells, sol_faces = finish(sums.reshape(devices, CZ), fields, faces)
    return (sol_cells.reshape(CX, CY, CZ), sol_faces)


def solution(mesh):
    placed = (
        P("gx", "gy", "gz"),
        P("gx", "gy", "gz"),
        P(("gx", "gy", "gz"), None),
        P(("gx", "gy", "gz"), None),
        P(("gx", "gy", "gz"), None, None, None),
        P(("gx", "gy", "gz"), None),
        P(("gx", "gy", "gz"), None, None),
        P(("gx", "gy", "gz"), None),
    )
    return jax.shard_map(
        local,
        mesh=mesh,
        in_specs=placed,
        out_specs=(P("gx", "gy", "gz"), P(("gx", "gy", "gz"), None)),
        check_vma=False,
    )
```

```python
import functools

import jax
import jax.numpy as jnp
from jax import lax
from jax.experimental import pallas as pl
from jax.experimental.pallas import tpu as pltpu
from jax.sharding import PartitionSpec as P

ITERS = 3
SHIFTS = (6.0, 3.0, 11.0)
SCALE = 0.125
CX, CY, CZ = 64, 32, 128
ROWS = CX * CY
TILES = 16
TILE = 128
FACES = TILES * TILE
SLOTS = 4
PER_OWNER = 4
f32 = jnp.float32
bf16 = jnp.bfloat16
VMEM = pl.BlockSpec(memory_space=pltpu.VMEM)
SMEM = pl.BlockSpec(memory_space=pltpu.SMEM)
HBM = pl.BlockSpec(memory_space=pltpu.HBM)
AXES = ("gx", "gy", "gz")
FIELD = jax.ShapeDtypeStruct((ROWS, CZ), f32)
ON_FACES = jax.ShapeDtypeStruct((TILES, TILE), f32)
CHUNKS = 4
PART = ROWS // CHUNKS
SIDE = ((CY, CZ), (CX, CZ), (TILES, TILE))
SIDES = tuple(jax.ShapeDtypeStruct(shape, f32) for shape in SIDE for _ in range(2))


def params(mib):
    return pltpu.CompilerParams(vmem_limit_bytes=mib << 20)


def split(x):
    high = x.astype(bf16)
    return high, (x - high.astype(f32)).astype(bf16)


def iota(shape, dim):
    return lax.broadcasted_iota(jnp.int32, shape, dim)


class Copies:
    def __init__(self, sems):
        self.sems = sems
        self.used = 0

    def start(self, source, target):
        copy = pltpu.make_async_copy(source, target, self.sems.at[self.used])
        self.used += 1
        copy.start()
        return copy


def outward(axis):
    odd = lax.rem(lax.axis_index(axis), 2)
    return 1 - odd, odd


def send_sides(copies, cells, edge_y, edge_z, sides):
    started = []
    for side, out in zip(outward("gx"), sides[0:2]):
        started.append(copies.start(cells.at[pl.ds(side * (ROWS - CY), CY), :], out))
    for edge, axis, outs in ((edge_y, "gy", sides[2:4]), (edge_z, "gz", sides[4:6])):
        for side, out in zip(outward(axis), outs):
            started.append(copies.start(edge.at[side], out))
    return started


def beside_z(group_z):
    z = lax.axis_index("gz")
    return z, lax.axis_index("gy") * group_z + z


def mark(rows, place):
    number = iota((ROWS, TILE), 0).astype(jnp.int16)
    one = jnp.ones((ROWS, TILE), bf16)
    zero = jnp.zeros((ROWS, TILE), bf16)

    def tile(i, carry):
        row = lax.shift_right_logical(place[pl.ds(i, 1), :], 7)
        row = jnp.broadcast_to(row, (16, TILE)).astype(jnp.int16)
        row = jnp.concatenate([row] * (ROWS // 16), axis=0)
        at = pl.ds(pl.multiple_of(i * TILE, TILE), TILE)
        rows[:, at] = jnp.where(number == row, one, zero)
        return carry

    lax.fori_loop(0, TILES, tile, 0)


def turn(u, wide, edge_z=None):
    def tile(i, carry):
        at = pl.ds(pl.multiple_of(i * TILE, TILE), TILE)
        part = u[at, :].T
        if edge_z is not None:
            edge_z[0, pl.ds(i, 1), :] = part[0:1, :]
            edge_z[1, pl.ds(i, 1), :] = part[CZ - 1 : CZ, :]
        high, low = split(part)
        wide[0:CZ, at] = high
        wide[CZ : 2 * CZ, at] = low
        return carry

    lax.fori_loop(0, TILES, tile, 0, unroll=4)


def look(rows, place, wide, under, beside=None):
    z = iota((CZ, TILE), 0)
    width = TILES // CHUNKS
    for c in range(CHUNKS):
        at = slice(c * width * TILE, (c + 1) * width * TILE)
        if beside is not None:
            beside(c)
        seen = jnp.dot(wide[...], rows[:, at], preferred_element_type=f32)
        both = seen[0:CZ] + seen[CZ : 2 * CZ]
        for h in range(width):
            i = c * width + h
            here = z == (place[i : i + 1, :] & (CZ - 1))
            part = jnp.where(here, both[:, h * TILE : (h + 1) * TILE], 0.0)
            under[i : i + 1, :] = jnp.sum(part, axis=0, keepdims=True)


def lay(s, under, place, spread):
    z = iota((CZ, TILE), 0)

    def tile(i, carry):
        at = pl.ds(pl.multiple_of(i * TILE, TILE), TILE)
        here = z == (place[pl.ds(i, 1), :] & (CZ - 1))
        high, low = split(1.0 * (under[pl.ds(i, 1), :] - s[pl.ds(i, 1), :]))
        spread[0:CZ, at] = jnp.where(here, high.astype(f32), 0.0).astype(bf16)
        spread[CZ : 2 * CZ, at] = jnp.where(here, low.astype(f32), 0.0).astype(bf16)
        return carry

    lax.fori_loop(0, TILES, tile, 0, unroll=4)


def meet(copies, shift, u, s, rows, place, heat, spread, under, base_out, under_out):
    puts = [copies.start(under, under_out)]
    lay(s, under, place, spread)
    for c in range(CHUNKS):
        at = pl.ds(c * PART, PART)
        sums = lax.dot_general(
            rows[at, :], spread[...], (((1,), (1,)), ((), ())), preferred_element_type=f32
        )
        heat[at, :] = (heat[at, :] + (6.0 - shift)) * u[at, :] + (
            sums[:, 0:CZ] + sums[:, CZ : 2 * CZ]
        )
        puts.append(copies.start(heat.at[at], base_out.at[at]))
    return puts


def wait_all(copies):
    for copy in copies:
        copy.wait()


def pack(group_z, sent, s, edge_z):
    z, mine = beside_z(group_z)
    value = s[...]
    low = edge_z[0]
    high = edge_z[1]
    for q in range(sent.shape[0]):
        sent[q, 0:TILES] = value
        sent[q, TILES : 2 * TILES] = jnp.where(mine - 1 == q, low, high)


def first_body(group_z, *refs):
    (u_in, s_in, place_in, heat_in, base_out, under_out, sent_out) = refs[:7]
    sides = refs[7:11]
    (u, s, place, heat, rows, under, sent, edge_y, edge_z, spread, wide, sems) = refs[11:]
    copies = Copies(sems)
    get_place = copies.start(place_in, place)
    get_u = copies.start(u_in, u)
    rest = [copies.start(s_in, s), copies.start(heat_in, heat)]
    get_place.wait()
    mark(rows, place)
    get_u.wait()
    for x in range(CX):
        edge_y[0, x : x + 1, :] = u[x * CY : x * CY + 1, :]
        edge_y[1, x : x + 1, :] = u[(x + 1) * CY - 1 : (x + 1) * CY, :]
    turn(u, wide, edge_z)
    puts = send_sides(copies, u, edge_y, edge_z, sides)
    wait_all(rest)
    pack(group_z, sent, s, edge_z)
    puts.append(copies.start(sent, sent_out))
    look(rows, place, wide, under)
    puts += meet(copies, SHIFTS[0], u, s, rows, place, heat, spread, under, base_out, under_out)
    wait_all(puts)


def field():
    return pltpu.VMEM((ROWS, CZ), f32)


def on_faces(dtype=f32):
    return pltpu.VMEM((TILES, TILE), dtype)


def one_hot():
    return pltpu.VMEM((ROWS, FACES), bf16)


def edge_buffers():
    return [pltpu.VMEM((2, CX, CZ), f32), pltpu.VMEM((2, TILES, TILE), f32)]


def call(body, name, ins, outs, scratch, sems, smem=0):
    specs = [SMEM] * smem + [HBM] * (len(ins) - smem)
    return pl.pallas_call(
        body,
        out_shape=tuple(outs),
        in_specs=specs,
        out_specs=(HBM,) * len(outs),
        scratch_shapes=list(scratch) + [pltpu.SemaphoreType.DMA((sems,))],
        compiler_params=params(64),
        name=name,
    )(*ins)


def parts():
    return [pltpu.VMEM((2 * CZ, FACES), bf16), pltpu.VMEM((2 * CZ, FACES), bf16)]


def first(group, group_z, u, s, place, heat):
    scratch = [field(), on_faces(), on_faces(jnp.int32), field(), one_hot(), on_faces()]
    scratch += [pltpu.VMEM((group, 2 * TILES, TILE), f32)] + edge_buffers() + parts()
    outs = (FIELD, ON_FACES, jax.ShapeDtypeStruct((group, 2 * TILES, TILE), f32)) + SIDES[:4]
    body = functools.partial(first_body, group_z)
    return call(body, "first_meet", (u, s, place, heat), outs, scratch, 15)


def stencil(step, chunk, u, base, edge_y, edge_z, new_block, sums):
    sub = iota((CY, CZ), 0)
    lane = iota((CY, CZ), 1)
    z = iota((CZ, TILE), 0)

    def block(i, sums):
        at_z = pl.ds(i, 1)
        facing = jnp.where(z == 0, edge_z[0, at_z, :], 0.0)
        facing = jnp.where(z == CZ - 1, edge_z[1, at_z, :], facing).T
        made = []
        for q in range(4):
            x = i * 4 + q
            row = pl.multiple_of(x * CY, CY)
            cur = u[pl.ds(row + CY, CY), :]
            beside = u[pl.ds(row, CY), :] + u[pl.ds(row + 2 * CY, CY), :]
            at_y = pl.ds(x, 1)
            low = jnp.where(sub == 0, edge_y[0, at_y, :], pltpu.roll(cur, 1, 0))
            high = jnp.where(sub == CY - 1, edge_y[1, at_y, :], pltpu.roll(cur, CY - 1, 0))
            beside = beside + (low + high)
            low = jnp.where(lane == 0, 0.0, pltpu.roll(cur, 1, 1))
            high = jnp.where(lane == CZ - 1, 0.0, pltpu.roll(cur, CZ - 1, 1))
            beside = beside + (low + high) + facing[q * CY : (q + 1) * CY, :]
            made.append((cur, (base[pl.ds(row, CY), :] - beside) * SCALE))
        return new_block(i, made, sums)

    count = TILES // CHUNKS
    return lax.fori_loop(chunk * count, (chunk + 1) * count, block, sums, unroll=2)


def emission(step, chunk, per_owner, slots, reads, factors, all_faces, emissive, own, under, new_faces, sums):
    eye = iota((TILE, TILE), 0) == iota((TILE, TILE), 1)

    def tile(i, sums):
        acc = None
        for k in range(SLOTS):
            slot = slots[k, i]
            owner = lax.shift_right_logical(slot, 2)
            column = owner * per_owner + reads[slot & (PER_OWNER - 1), owner]
            term = factors[i, k] * all_faces[pl.ds(column, 1), :]
            acc = term if acc is None else acc + term
        row = jnp.sum(acc, axis=1, keepdims=True)
        flux = jnp.sum(jnp.where(eye, row, 0.0), axis=0, keepdims=True)
        at = pl.ds(i, 1)
        mine = own[at, :]
        e = emissive[at, :]
        new = ((1.0 - SHIFTS[step] + e) * mine - under[at, :] - e * flux) * SCALE
        return new_faces(at, mine, new, sums)

    count = TILES // CHUNKS
    return lax.fori_loop(chunk * count, (chunk + 1) * count, tile, sums, unroll=count)


def get_halos(copies, group_z, halos, received, u, edge_y, edge_z):
    started = []
    for side, halo in zip(outward("gx"), halos[0:2]):
        started.append(copies.start(halo, u.at[pl.ds(side * (ROWS + CY), CY), :]))
    for edge, axis, pair in ((edge_y, "gy", halos[2:4]), (edge_z, "gz", halos[4:6])):
        for side, halo in zip(outward(axis), pair):
            started.append(copies.start(halo, edge.at[side]))
    if len(halos) == 4:
        z, mine = beside_z(group_z)
        for side, (there, peer) in enumerate(((z > 0, mine - 1), (z < group_z - 1, mine + 1))):
            row = jnp.where(there, peer, mine) * (2 * TILES) + TILES
            started.append(copies.start(received.at[pl.ds(row, TILES), :], edge_z.at[side]))
    return started


def clear_ends(group_z, halos, edge_z):
    if len(halos) == 4:
        z = lax.axis_index("gz")
        for side, there in enumerate((z > 0, z < group_z - 1)):
            edge_z[side] = jnp.where(there, edge_z[side], 0.0)


def in_chunks(copies, source, target, offset=0):
    part = source.shape[0] // CHUNKS
    return [
        copies.start(source.at[pl.ds(c * part, part)], target.at[pl.ds(offset + c * part, part)])
        for c in range(CHUNKS)
    ]


def middle_body(step, group_z, count, *refs):
    (slots, reads, u_in, base_in, all_in, factors_in, emissive_in, under_in, s_in) = refs[:9]
    (place_in, heat_in) = refs[9:11]
    halos, refs = refs[11 : 11 + count], refs[11 + count :]
    (u_out, s_out, sent_out, base_out, under_out) = refs[:5]
    sides = refs[5:9]
    (u, base, all_faces, factors, emissive, under, s, place, heat) = refs[9:18]
    (new_u, new_s, new_under, sent, halo_y, halo_z, edge_y, edge_z) = refs[18:26]
    (rows, spread, wide, sems) = refs[26:]
    copies = Copies(sems)
    get_place = copies.start(place_in, place)
    get_u = in_chunks(copies, u_in, u, CY)
    gets = get_halos(copies, group_z, halos, all_in, u, halo_y, halo_z)
    get_base = in_chunks(copies, base_in, base)
    pairs = ((all_in, all_faces), (emissive_in, emissive), (under_in, under), (s_in, s))
    get_faces = [copies.start(a, b) for a, b in pairs]
    get_factors = in_chunks(copies, factors_in, factors)
    get_heat = copies.start(heat_in, heat)
    get_place.wait()
    mark(rows, place)
    wait_all(get_u + gets)
    clear_ends(group_z, halos, halo_z)

    def new_block(i, made, sums):
        for q, (_, new) in enumerate(made):
            new_u[pl.ds(pl.multiple_of(i * TILE + q * CY, CY), CY), :] = new
            edge_y[0, pl.ds(i * 4 + q, 1), :] = new[0:1, :]
            edge_y[1, pl.ds(i * 4 + q, 1), :] = new[CY - 1 : CY, :]
        return sums

    def new_faces(at, mine, new, sums):
        new_s[at, :] = new
        return sums

    puts = []
    for c in range(CHUNKS):
        get_base[c].wait()
        stencil(step, c, u, base, halo_y, halo_z, new_block, 0)
        at = pl.ds(c * PART, PART)
        puts.append(copies.start(new_u.at[at], u_out.at[at]))
    turn(new_u, wide, edge_z)
    puts += send_sides(copies, new_u, edge_y, edge_z, sides)
    wait_all(get_faces + get_factors)
    per_owner = all_faces.shape[0] // sent.shape[0]

    def radiate(c):
        emission(
            step, c, per_owner, slots, reads, factors, all_faces, emissive, s, under, new_faces, 0
        )

    look(rows, place, wide, new_under, radiate)
    puts.append(copies.start(new_s, s_out))
    pack(group_z, sent, new_s, edge_z)
    puts.append(copies.start(sent, sent_out))
    get_heat.wait()
    puts += meet(
        copies, SHIFTS[step + 1], new_u, new_s, rows, place, heat, spread, new_under,
        base_out, under_out,
    )
    wait_all(puts)


def middle(
    step, group, group_z, slots, reads, u, base, all_faces, factors, emissive, under, s, place, heat,
    halos,
):
    scratch = [pltpu.VMEM((ROWS + 2 * CY, CZ), f32), field()] + face_buffers(all_faces, factors)
    scratch += [on_faces(jnp.int32), field(), field(), on_faces(), on_faces()]
    scratch += [pltpu.VMEM((group, 2 * TILES, TILE), f32)]
    scratch += edge_buffers() + edge_buffers() + [one_hot()] + parts()
    body = functools.partial(middle_body, step, group_z, len(halos))
    outs = (FIELD, ON_FACES, jax.ShapeDtypeStruct((group, 2 * TILES, TILE), f32), FIELD, ON_FACES)
    ins = (slots, reads, u, base, all_faces, factors, emissive, under, s, place, heat, *halos)
    return call(body, "apply_and_meet", ins, outs + SIDES[:4], scratch, 40, 2)


def face_buffers(all_faces, factors):
    shapes = [pltpu.VMEM(all_faces.shape, f32), pltpu.VMEM(factors.shape, f32)]
    return shapes + [on_faces(), on_faces(), on_faces()]


def products(vectors):
    return [vectors[a] * vectors[b] for b in range(ITERS + 1) for a in range(b + 1)]


PAIRS = (ITERS + 1) * (ITERS + 2) // 2


def last_body(group_z, *refs):
    (slots, reads, u_in, base_in, all_in, factors_in, emissive_in, under_in, s_in) = refs[:9]
    (u0_in, u1_in, s0_in, s1_in) = refs[9:13]
    halos = refs[13:17]
    sent_out = refs[17]
    (u, base, u0, u1, all_faces, factors, emissive, under, s, s0, s1) = refs[18:29]
    (halo_y, halo_z, sent, sems) = refs[29:]
    copies = Copies(sems)
    get_u = in_chunks(copies, u_in, u, CY)
    gets = get_halos(copies, group_z, halos, all_in, u, halo_y, halo_z)
    fields = []
    for c in range(CHUNKS):
        at = pl.ds(c * PART, PART)
        pairs = ((base_in, base), (u0_in, u0), (u1_in, u1))
        fields.append([copies.start(a.at[at], b.at[at]) for a, b in pairs])
    pairs = ((all_in, all_faces), (emissive_in, emissive), (under_in, under), (s_in, s))
    pairs += ((s0_in, s0), (s1_in, s1))
    small = [copies.start(a, b) for a, b in pairs]
    get_factors = in_chunks(copies, factors_in, factors)
    wait_all(get_u + gets)
    clear_ends(group_z, halos, halo_z)

    def new_block(i, made, sums):
        for q, (cur, new) in enumerate(made):
            at = pl.ds(pl.multiple_of(i * TILE + q * CY, CY), CY)
            terms = products([u0[at, :], u1[at, :], cur, new])
            sums = tuple(
                acc + ((p[0:8] + p[8:16]) + (p[16:24] + p[24:32])) for acc, p in zip(sums, terms)
            )
        return sums

    def new_faces(at, mine, new, sums):
        terms = products([s0[at, :], s1[at, :], mine, new])
        return tuple(acc + p for acc, p in zip(sums, terms))

    by_cells = tuple(jnp.zeros((8, CZ), f32) for _ in range(PAIRS))
    for c, parts in enumerate(fields):
        wait_all(parts)
        by_cells = stencil(ITERS - 1, c, u, base, halo_y, halo_z, new_block, by_cells)
    wait_all(small)
    by_faces = tuple(jnp.zeros((1, TILE), f32) for _ in range(PAIRS))
    for c in range(CHUNKS):
        get_factors[c].wait()
        by_faces = emission(
            ITERS - 1, c, 2 * TILES, slots, reads, factors, all_faces, emissive, s, under, new_faces,
            by_faces,
        )
    spot = iota((1, CZ), 1)
    row = jnp.zeros((1, CZ), f32)
    for d in range(PAIRS):
        both = jnp.sum(by_cells[d], axis=0, keepdims=True) + by_faces[d]
        row = jnp.where(spot == d, jnp.sum(both, axis=1, keepdims=True), row)
    for q in range(sent.shape[0] // 8):
        sent[q * 8 : (q + 1) * 8, :] = jnp.broadcast_to(row, (8, CZ))
    copies.start(sent, sent_out).wait()


def last(devices, group_z, slots, reads, u, base, all_faces, factors, emissive, under, s, u0, u1, s0, s1, halos):
    scratch = [pltpu.VMEM((ROWS + 2 * CY, CZ), f32), field(), field(), field()]
    scratch += face_buffers(all_faces, factors) + [on_faces(), on_faces()]
    scratch += edge_buffers() + [pltpu.VMEM((devices, CZ), f32)]
    ins = (slots, reads, u, base, all_faces, factors, emissive, under, s, u0, u1, s0, s1, *halos)
    outs = (jax.ShapeDtypeStruct((devices, CZ), f32),)
    return call(functools.partial(last_body, group_z), "apply_and_reduce", ins, outs, scratch, 33, 2)[0]


def finish_body(*refs):
    (parts_in, u0_in, u1_in, u2_in, s0_in, s1_in, s2_in, out_u, out_s) = refs[:9]
    (parts, u0, u1, u2, s0, s1, s2, sems) = refs[9:]
    copies = Copies(sems)
    get_parts = copies.start(parts_in, parts)
    get_s = [copies.start(a, b) for a, b in ((s0_in, s0), (s1_in, s1), (s2_in, s2))]
    get_u = []
    for c in range(CHUNKS):
        at = pl.ds(c * PART, PART)
        pairs = ((u0_in, u0), (u1_in, u1), (u2_in, u2))
        get_u.append([copies.start(a.at[at], b.at[at]) for a, b in pairs])
    get_parts.wait()
    total = jnp.sum(parts[...], axis=0, keepdims=True)
    entry = [total[:, d : d + 1] for d in range(10)]
    (g00, g01, g11, g02, g12, g22, g03, g13, g23, g33) = entry
    gram = [
        [g00, g01, g02, g03],
        [g01, g11, g12, g13],
        [g02, g12, g22, g23],
        [g03, g13, g23, g33],
    ]
    grow = 1.0 / SCALE
    image = [
        [SHIFTS[j] * gram[j][b] + grow * gram[j + 1][b] for b in range(ITERS + 1)]
        for j in range(ITERS)
    ]
    normal = [
        [SHIFTS[b] * image[a][b] + grow * image[a][b + 1] for b in range(ITERS)]
        for a in range(ITERS)
    ]
    target = [image[a][0] for a in range(ITERS)]
    for col in range(ITERS):
        for row in range(col + 1, ITERS):
            factor = normal[row][col] / normal[col][col]
            normal[row] = [normal[row][b] - factor * normal[col][b] for b in range(ITERS)]
            target[row] = target[row] - factor * target[col]
    coeffs = [None] * ITERS
    for row in range(ITERS - 1, -1, -1):
        acc = target[row]
        for b in range(row + 1, ITERS):
            acc = acc - normal[row][b] * coeffs[b]
        coeffs[row] = acc / normal[row][row]
    wide = [jnp.broadcast_to(c, (8, TILE)) for c in coeffs]

    def mix(ref, others):
        def rows(i, carry):
            at = pl.ds(pl.multiple_of(i * 8, 8), 8)
            ref[at, :] = (
                wide[0] * ref[at, :] + wide[1] * others[0][at, :] + wide[2] * others[1][at, :]
            )
            return carry

        return rows

    wait_all(get_s)
    lax.fori_loop(0, TILES // 8, mix(s0, (s1, s2)), 0, unroll=2)
    puts = [copies.start(s0, out_s)]
    for c, gets in enumerate(get_u):
        wait_all(gets)
        lax.fori_loop(c * PART // 8, (c + 1) * PART // 8, mix(u0, (u1, u2)), 0, unroll=8)
        at = pl.ds(c * PART, PART)
        puts.append(copies.start(u0.at[at], out_u.at[at]))
    wait_all(puts)


def finish(parts, fields, faces):
    scratch = [pltpu.VMEM(parts.shape, f32)] + [field()] * 3 + [on_faces()] * 3
    return call(finish_body, "finish", (parts, *fields, *faces), (FIELD, ON_FACES), scratch, 21)


def exchanged(sides):
    halos = []
    for axis, pair in zip(AXES, [sides[n : n + 2] for n in range(0, len(sides), 2)]):
        size = lax.axis_size(axis)
        even = [(i, i ^ 1) for i in range(size)]
        odd = [(i, i + 1) for i in range(1, size - 1, 2)]
        odd += [(b, a) for a, b in odd]
        halos += [lax.ppermute(pair[0], axis, even), lax.ppermute(pair[1], axis, odd)]
    return halos


def local(
    rhs_cells, heat_diag, rhs_faces, emissive, view_factors, tile_slots, read_lists, face_cells
):
    slab = ("gy", "gz")
    group = lax.axis_size(slab)
    group_z = lax.axis_size("gz")
    devices = lax.axis_size(AXES)
    slots = tile_slots.T
    reads = read_lists[0].T
    flat = (ROWS, CZ)
    fields, faces = [rhs_cells.reshape(flat)], [rhs_faces]
    heat = heat_diag.reshape(flat)
    for j in range(ITERS):
        u, s = fields[j], faces[j]
        if j == 0:
            base, under, sent, *sides = first(group, group_z, u, s, face_cells, heat)
            halos = exchanged(sides)
        all_faces = lax.all_to_all(sent, slab, 0, 0, tiled=True).reshape(-1, TILE)
        given = (slots, reads, u, base, all_faces, view_factors, emissive, under, s)
        if j + 1 < ITERS:
            u, s, sent, base, under, *sides = middle(
                j, group, group_z, *given, face_cells, heat, halos
            )
            halos = exchanged(sides)
            fields.append(u)
            faces.append(s)
        else:
            dots = last(devices, group_z, *given, *fields[:j], *faces[:j], halos)
    sums = lax.all_to_all(dots[:, None, :], AXES, 0, 0, tiled=True)
    sol_cells, sol_faces = finish(sums.reshape(devices, CZ), fields, faces)
    return (sol_cells.reshape(CX, CY, CZ), sol_faces)


def solution(mesh):
    placed = (
        P("gx", "gy", "gz"),
        P("gx", "gy", "gz"),
        P(("gx", "gy", "gz"), None),
        P(("gx", "gy", "gz"), None),
        P(("gx", "gy", "gz"), None, None, None),
        P(("gx", "gy", "gz"), None),
        P(("gx", "gy", "gz"), None, None),
        P(("gx", "gy", "gz"), None),
    )
    return jax.shard_map(
        local,
        mesh=mesh,
        in_specs=placed,
        out_specs=(P("gx", "gy", "gz"), P(("gx", "gy", "gz"), None)),
        check_vma=False,
    )
```

```python
import functools

import jax
import jax.numpy as jnp
from jax import lax
from jax.experimental import pallas as pl
from jax.experimental.pallas import tpu as pltpu
from jax.sharding import PartitionSpec as P

ITERS = 3
SHIFTS = (6.0, 3.0, 11.0)
SCALE = 0.125
CX, CY, CZ = 64, 32, 128
ROWS = CX * CY
TILES = 16
TILE = 128
FACES = TILES * TILE
SLOTS = 4
PER_OWNER = 4
f32 = jnp.float32
bf16 = jnp.bfloat16
VMEM = pl.BlockSpec(memory_space=pltpu.VMEM)
SMEM = pl.BlockSpec(memory_space=pltpu.SMEM)
HBM = pl.BlockSpec(memory_space=pltpu.HBM)
AXES = ("gx", "gy", "gz")
FIELD = jax.ShapeDtypeStruct((ROWS, CZ), f32)
ON_FACES = jax.ShapeDtypeStruct((TILES, TILE), f32)
CHUNKS = 4
PART = ROWS // CHUNKS
SIDE = ((CY, CZ), (CX, CZ), (TILES, TILE))
SIDES = tuple(jax.ShapeDtypeStruct(shape, f32) for shape in SIDE for _ in range(2))


def params(mib):
    return pltpu.CompilerParams(vmem_limit_bytes=mib << 20)


def split(x):
    high = x.astype(bf16)
    return high, (x - high.astype(f32)).astype(bf16)


def iota(shape, dim):
    return lax.broadcasted_iota(jnp.int32, shape, dim)


class Copies:
    def __init__(self, sems):
        self.sems = sems
        self.used = 0

    def start(self, source, target):
        copy = pltpu.make_async_copy(source, target, self.sems.at[self.used])
        self.used += 1
        copy.start()
        return copy


def outward(axis):
    odd = lax.rem(lax.axis_index(axis), 2)
    return 1 - odd, odd


def send_sides(copies, cells, edge_y, edge_z, sides):
    started = []
    for side, out in zip(outward("gx"), sides[0:2]):
        started.append(copies.start(cells.at[pl.ds(side * (ROWS - CY), CY), :], out))
    for edge, axis, outs in ((edge_y, "gy", sides[2:4]), (edge_z, "gz", sides[4:6])):
        for side, out in zip(outward(axis), outs):
            started.append(copies.start(edge.at[side], out))
    return started


def beside_z(group_z):
    z = lax.axis_index("gz")
    return z, lax.axis_index("gy") * group_z + z


def mark(rows, place):
    number = iota((ROWS, TILE), 0).astype(jnp.int16)
    one = jnp.ones((ROWS, TILE), bf16)
    zero = jnp.zeros((ROWS, TILE), bf16)

    def tile(i, carry):
        row = lax.shift_right_logical(place[pl.ds(i, 1), :], 7)
        row = jnp.broadcast_to(row, (16, TILE)).astype(jnp.int16)
        row = jnp.concatenate([row] * (ROWS // 16), axis=0)
        at = pl.ds(pl.multiple_of(i * TILE, TILE), TILE)
        rows[:, at] = jnp.where(number == row, one, zero)
        return carry

    lax.fori_loop(0, TILES, tile, 0)


def turn(u, wide, edge_z=None):
    def tile(i, carry):
        at = pl.ds(pl.multiple_of(i * TILE, TILE), TILE)
        part = u[at, :].T
        if edge_z is not None:
            edge_z[0, pl.ds(i, 1), :] = part[0:1, :]
            edge_z[1, pl.ds(i, 1), :] = part[CZ - 1 : CZ, :]
        high, low = split(part)
        wide[0:CZ, at] = high
        wide[CZ : 2 * CZ, at] = low
        return carry

    lax.fori_loop(0, TILES, tile, 0, unroll=4)


def look(rows, place, wide, under, beside=None):
    z = iota((CZ, TILE), 0)
    width = TILES // CHUNKS
    for c in range(CHUNKS):
        at = slice(c * width * TILE, (c + 1) * width * TILE)
        if beside is not None:
            beside(c)
        seen = jnp.dot(wide[...], rows[:, at], preferred_element_type=f32)
        both = seen[0:CZ] + seen[CZ : 2 * CZ]
        for h in range(width):
            i = c * width + h
            here = z == (place[i : i + 1, :] & (CZ - 1))
            part = jnp.where(here, both[:, h * TILE : (h + 1) * TILE], 0.0)
            under[i : i + 1, :] = jnp.sum(part, axis=0, keepdims=True)


def lay(s, under, place, spread):
    z = iota((CZ, TILE), 0)

    def tile(i, carry):
        at = pl.ds(pl.multiple_of(i * TILE, TILE), TILE)
        here = z == (place[pl.ds(i, 1), :] & (CZ - 1))
        high, low = split(1.0 * (under[pl.ds(i, 1), :] - s[pl.ds(i, 1), :]))
        spread[0:CZ, at] = jnp.where(here, high.astype(f32), 0.0).astype(bf16)
        spread[CZ : 2 * CZ, at] = jnp.where(here, low.astype(f32), 0.0).astype(bf16)
        return carry

    lax.fori_loop(0, TILES, tile, 0, unroll=4)


def meet(copies, shift, u, s, rows, place, heat, spread, under, base_out, under_out):
    puts = [copies.start(under, under_out)]
    lay(s, under, place, spread)
    for c in range(CHUNKS):
        at = pl.ds(c * PART, PART)
        sums = lax.dot_general(
            rows[at, :], spread[...], (((1,), (1,)), ((), ())), preferred_element_type=f32
        )
        heat[at, :] = (heat[at, :] + (6.0 - shift)) * u[at, :] + (
            sums[:, 0:CZ] + sums[:, CZ : 2 * CZ]
        )
        puts.append(copies.start(heat.at[at], base_out.at[at]))
    return puts


def wait_all(copies):
    for copy in copies:
        copy.wait()


def pack(group_z, sent, s, edge_z):
    z, mine = beside_z(group_z)
    value = s[...]
    low = edge_z[0]
    high = edge_z[1]
    for q in range(sent.shape[0]):
        sent[q, 0:TILES] = value
        sent[q, TILES : 2 * TILES] = jnp.where(mine - 1 == q, low, high)


def first_body(group_z, *refs):
    (u_in, s_in, place_in, heat_in, base_out, under_out, sent_out) = refs[:7]
    sides = refs[7:11]
    (u, s, place, heat, rows, under, sent, edge_y, edge_z, spread, wide, sems) = refs[11:]
    copies = Copies(sems)
    get_place = copies.start(place_in, place)
    get_u = copies.start(u_in, u)
    rest = [copies.start(s_in, s), copies.start(heat_in, heat)]
    get_place.wait()
    mark(rows, place)
    get_u.wait()
    for x in range(CX):
        edge_y[0, x : x + 1, :] = u[x * CY : x * CY + 1, :]
        edge_y[1, x : x + 1, :] = u[(x + 1) * CY - 1 : (x + 1) * CY, :]
    turn(u, wide, edge_z)
    puts = send_sides(copies, u, edge_y, edge_z, sides)
    wait_all(rest)
    pack(group_z, sent, s, edge_z)
    puts.append(copies.start(sent, sent_out))
    look(rows, place, wide, under)
    puts += meet(copies, SHIFTS[0], u, s, rows, place, heat, spread, under, base_out, under_out)
    wait_all(puts)


def field():
    return pltpu.VMEM((ROWS, CZ), f32)


def on_faces(dtype=f32):
    return pltpu.VMEM((TILES, TILE), dtype)


def one_hot():
    return pltpu.VMEM((ROWS, FACES), bf16)


def edge_buffers():
    return [pltpu.VMEM((2, CX, CZ), f32), pltpu.VMEM((2, TILES, TILE), f32)]


def call(body, name, ins, outs, scratch, sems, smem=0):
    specs = [SMEM] * smem + [HBM] * (len(ins) - smem)
    return pl.pallas_call(
        body,
        out_shape=tuple(outs),
        in_specs=specs,
        out_specs=(HBM,) * len(outs),
        scratch_shapes=list(scratch) + [pltpu.SemaphoreType.DMA((sems,))],
        compiler_params=params(64),
        name=name,
    )(*ins)


def parts():
    return [pltpu.VMEM((2 * CZ, FACES), bf16), pltpu.VMEM((2 * CZ, FACES), bf16)]


def first(group, group_z, u, s, place, heat):
    scratch = [field(), on_faces(), on_faces(jnp.int32), field(), one_hot(), on_faces()]
    scratch += [pltpu.VMEM((group, 2 * TILES, TILE), f32)] + edge_buffers() + parts()
    outs = (FIELD, ON_FACES, jax.ShapeDtypeStruct((group, 2 * TILES, TILE), f32)) + SIDES[:4]
    body = functools.partial(first_body, group_z)
    return call(body, "first_meet", (u, s, place, heat), outs, scratch, 15)


def stencil(step, chunk, u, base, edge_y, edge_z, new_block, sums):
    sub = iota((CY, CZ), 0)
    lane = iota((CY, CZ), 1)
    z = iota((CZ, TILE), 0)

    def block(i, sums):
        at_z = pl.ds(i, 1)
        facing = jnp.where(z == 0, edge_z[0, at_z, :], 0.0)
        facing = jnp.where(z == CZ - 1, edge_z[1, at_z, :], facing).T
        made = []
        for q in range(4):
            x = i * 4 + q
            row = pl.multiple_of(x * CY, CY)
            cur = u[pl.ds(row + CY, CY), :]
            beside = u[pl.ds(row, CY), :] + u[pl.ds(row + 2 * CY, CY), :]
            at_y = pl.ds(x, 1)
            low = jnp.where(sub == 0, edge_y[0, at_y, :], pltpu.roll(cur, 1, 0))
            high = jnp.where(sub == CY - 1, edge_y[1, at_y, :], pltpu.roll(cur, CY - 1, 0))
            beside = beside + (low + high)
            low = jnp.where(lane == 0, 0.0, pltpu.roll(cur, 1, 1))
            high = jnp.where(lane == CZ - 1, 0.0, pltpu.roll(cur, CZ - 1, 1))
            beside = beside + (low + high) + facing[q * CY : (q + 1) * CY, :]
            made.append((cur, (base[pl.ds(row, CY), :] - beside) * SCALE))
        return new_block(i, made, sums)

    count = TILES // CHUNKS
    return lax.fori_loop(chunk * count, (chunk + 1) * count, block, sums, unroll=count)


def emission(step, chunk, per_owner, slots, reads, factors, all_faces, emissive, own, under, new_faces, sums):
    eye = iota((TILE, TILE), 0) == iota((TILE, TILE), 1)

    def tile(i, sums):
        acc = None
        for k in range(SLOTS):
            slot = slots[k, i]
            owner = lax.shift_right_logical(slot, 2)
            column = owner * per_owner + reads[slot & (PER_OWNER - 1), owner]
            term = factors[i, k] * all_faces[pl.ds(column, 1), :]
            acc = term if acc is None else acc + term
        row = jnp.sum(acc, axis=1, keepdims=True)
        flux = jnp.sum(jnp.where(eye, row, 0.0), axis=0, keepdims=True)
        at = pl.ds(i, 1)
        mine = own[at, :]
        e = emissive[at, :]
        new = ((1.0 - SHIFTS[step] + e) * mine - under[at, :] - e * flux) * SCALE
        return new_faces(at, mine, new, sums)

    count = TILES // CHUNKS
    return lax.fori_loop(chunk * count, (chunk + 1) * count, tile, sums, unroll=count)


def get_halos(copies, group_z, halos, received, u, edge_y, edge_z):
    started = []
    for side, halo in zip(outward("gx"), halos[0:2]):
        started.append(copies.start(halo, u.at[pl.ds(side * (ROWS + CY), CY), :]))
    for edge, axis, pair in ((edge_y, "gy", halos[2:4]), (edge_z, "gz", halos[4:6])):
        for side, halo in zip(outward(axis), pair):
            started.append(copies.start(halo, edge.at[side]))
    if len(halos) == 4:
        z, mine = beside_z(group_z)
        for side, (there, peer) in enumerate(((z > 0, mine - 1), (z < group_z - 1, mine + 1))):
            row = jnp.where(there, peer, mine) * (2 * TILES) + TILES
            started.append(copies.start(received.at[pl.ds(row, TILES), :], edge_z.at[side]))
    return started


def clear_ends(group_z, halos, edge_z):
    if len(halos) == 4:
        z = lax.axis_index("gz")
        for side, there in enumerate((z > 0, z < group_z - 1)):
            edge_z[side] = jnp.where(there, edge_z[side], 0.0)


def in_chunks(copies, source, target, offset=0):
    part = source.shape[0] // CHUNKS
    return [
        copies.start(source.at[pl.ds(c * part, part)], target.at[pl.ds(offset + c * part, part)])
        for c in range(CHUNKS)
    ]


def middle_body(step, group_z, count, *refs):
    (slots, reads, u_in, base_in, all_in, factors_in, emissive_in, under_in, s_in) = refs[:9]
    (place_in, heat_in) = refs[9:11]
    halos, refs = refs[11 : 11 + count], refs[11 + count :]
    (u_out, s_out, sent_out, base_out, under_out) = refs[:5]
    sides = refs[5:9]
    (u, base, all_faces, factors, emissive, under, s, place, heat) = refs[9:18]
    (new_u, new_s, new_under, sent, halo_y, halo_z, edge_y, edge_z) = refs[18:26]
    (rows, spread, wide, sems) = refs[26:]
    copies = Copies(sems)
    get_place = copies.start(place_in, place)
    get_u = in_chunks(copies, u_in, u, CY)
    gets = get_halos(copies, group_z, halos, all_in, u, halo_y, halo_z)
    get_base = in_chunks(copies, base_in, base)
    pairs = ((all_in, all_faces), (emissive_in, emissive), (under_in, under), (s_in, s))
    get_faces = [copies.start(a, b) for a, b in pairs]
    get_factors = in_chunks(copies, factors_in, factors)
    get_heat = copies.start(heat_in, heat)
    get_place.wait()
    mark(rows, place)
    wait_all(get_u + gets)
    clear_ends(group_z, halos, halo_z)

    def new_block(i, made, sums):
        for q, (_, new) in enumerate(made):
            new_u[pl.ds(pl.multiple_of(i * TILE + q * CY, CY), CY), :] = new
            edge_y[0, pl.ds(i * 4 + q, 1), :] = new[0:1, :]
            edge_y[1, pl.ds(i * 4 + q, 1), :] = new[CY - 1 : CY, :]
        return sums

    def new_faces(at, mine, new, sums):
        new_s[at, :] = new
        return sums

    puts = []
    for c in range(CHUNKS):
        get_base[c].wait()
        stencil(step, c, u, base, halo_y, halo_z, new_block, 0)
        at = pl.ds(c * PART, PART)
        puts.append(copies.start(new_u.at[at], u_out.at[at]))
    turn(new_u, wide, edge_z)
    puts += send_sides(copies, new_u, edge_y, edge_z, sides)
    wait_all(get_faces + get_factors)
    per_owner = all_faces.shape[0] // sent.shape[0]

    def radiate(c):
        emission(
            step, c, per_owner, slots, reads, factors, all_faces, emissive, s, under, new_faces, 0
        )

    look(rows, place, wide, new_under, radiate)
    puts.append(copies.start(new_s, s_out))
    pack(group_z, sent, new_s, edge_z)
    puts.append(copies.start(sent, sent_out))
    get_heat.wait()
    puts += meet(
        copies, SHIFTS[step + 1], new_u, new_s, rows, place, heat, spread, new_under,
        base_out, under_out,
    )
    wait_all(puts)


def middle(
    step, group, group_z, slots, reads, u, base, all_faces, factors, emissive, under, s, place, heat,
    halos,
):
    scratch = [pltpu.VMEM((ROWS + 2 * CY, CZ), f32), field()] + face_buffers(all_faces, factors)
    scratch += [on_faces(jnp.int32), field(), field(), on_faces(), on_faces()]
    scratch += [pltpu.VMEM((group, 2 * TILES, TILE), f32)]
    scratch += edge_buffers() + edge_buffers() + [one_hot()] + parts()
    body = functools.partial(middle_body, step, group_z, len(halos))
    outs = (FIELD, ON_FACES, jax.ShapeDtypeStruct((group, 2 * TILES, TILE), f32), FIELD, ON_FACES)
    ins = (slots, reads, u, base, all_faces, factors, emissive, under, s, place, heat, *halos)
    return call(body, "apply_and_meet", ins, outs + SIDES[:4], scratch, 40, 2)


def face_buffers(all_faces, factors):
    shapes = [pltpu.VMEM(all_faces.shape, f32), pltpu.VMEM(factors.shape, f32)]
    return shapes + [on_faces(), on_faces(), on_faces()]


def products(vectors):
    return [vectors[a] * vectors[b] for b in range(ITERS + 1) for a in range(b + 1)]


PAIRS = (ITERS + 1) * (ITERS + 2) // 2


def last_body(group_z, *refs):
    (slots, reads, u_in, base_in, all_in, factors_in, emissive_in, under_in, s_in) = refs[:9]
    (u0_in, u1_in, s0_in, s1_in) = refs[9:13]
    halos = refs[13:17]
    sent_out = refs[17]
    (u, base, u0, u1, all_faces, factors, emissive, under, s, s0, s1) = refs[18:29]
    (halo_y, halo_z, sent, sems) = refs[29:]
    copies = Copies(sems)
    get_u = in_chunks(copies, u_in, u, CY)
    gets = get_halos(copies, group_z, halos, all_in, u, halo_y, halo_z)
    fields = []
    for c in range(CHUNKS):
        at = pl.ds(c * PART, PART)
        pairs = ((base_in, base), (u0_in, u0), (u1_in, u1))
        fields.append([copies.start(a.at[at], b.at[at]) for a, b in pairs])
    pairs = ((all_in, all_faces), (emissive_in, emissive), (under_in, under), (s_in, s))
    pairs += ((s0_in, s0), (s1_in, s1))
    small = [copies.start(a, b) for a, b in pairs]
    get_factors = in_chunks(copies, factors_in, factors)
    wait_all(get_u + gets)
    clear_ends(group_z, halos, halo_z)

    def new_block(i, made, sums):
        for q, (cur, new) in enumerate(made):
            at = pl.ds(pl.multiple_of(i * TILE + q * CY, CY), CY)
            terms = products([u0[at, :], u1[at, :], cur, new])
            sums = tuple(
                acc + ((p[0:8] + p[8:16]) + (p[16:24] + p[24:32])) for acc, p in zip(sums, terms)
            )
        return sums

    def new_faces(at, mine, new, sums):
        terms = products([s0[at, :], s1[at, :], mine, new])
        return tuple(acc + p for acc, p in zip(sums, terms))

    by_cells = tuple(jnp.zeros((8, CZ), f32) for _ in range(PAIRS))
    for c, parts in enumerate(fields):
        wait_all(parts)
        by_cells = stencil(ITERS - 1, c, u, base, halo_y, halo_z, new_block, by_cells)
    wait_all(small)
    by_faces = tuple(jnp.zeros((1, TILE), f32) for _ in range(PAIRS))
    for c in range(CHUNKS):
        get_factors[c].wait()
        by_faces = emission(
            ITERS - 1, c, 2 * TILES, slots, reads, factors, all_faces, emissive, s, under, new_faces,
            by_faces,
        )
    spot = iota((1, CZ), 1)
    row = jnp.zeros((1, CZ), f32)
    for d in range(PAIRS):
        both = jnp.sum(by_cells[d], axis=0, keepdims=True) + by_faces[d]
        row = jnp.where(spot == d, jnp.sum(both, axis=1, keepdims=True), row)
    for q in range(sent.shape[0] // 8):
        sent[q * 8 : (q + 1) * 8, :] = jnp.broadcast_to(row, (8, CZ))
    copies.start(sent, sent_out).wait()


def last(devices, group_z, slots, reads, u, base, all_faces, factors, emissive, under, s, u0, u1, s0, s1, halos):
    scratch = [pltpu.VMEM((ROWS + 2 * CY, CZ), f32), field(), field(), field()]
    scratch += face_buffers(all_faces, factors) + [on_faces(), on_faces()]
    scratch += edge_buffers() + [pltpu.VMEM((devices, CZ), f32)]
    ins = (slots, reads, u, base, all_faces, factors, emissive, under, s, u0, u1, s0, s1, *halos)
    outs = (jax.ShapeDtypeStruct((devices, CZ), f32),)
    return call(functools.partial(last_body, group_z), "apply_and_reduce", ins, outs, scratch, 33, 2)[0]


def finish_body(*refs):
    (parts_in, u0_in, u1_in, u2_in, s0_in, s1_in, s2_in, out_u, out_s) = refs[:9]
    (parts, u0, u1, u2, s0, s1, s2, sems) = refs[9:]
    copies = Copies(sems)
    get_parts = copies.start(parts_in, parts)
    get_s = [copies.start(a, b) for a, b in ((s0_in, s0), (s1_in, s1), (s2_in, s2))]
    get_u = []
    for c in range(CHUNKS):
        at = pl.ds(c * PART, PART)
        pairs = ((u0_in, u0), (u1_in, u1), (u2_in, u2))
        get_u.append([copies.start(a.at[at], b.at[at]) for a, b in pairs])
    get_parts.wait()
    total = jnp.sum(parts[...], axis=0, keepdims=True)
    entry = [total[:, d : d + 1] for d in range(10)]
    (g00, g01, g11, g02, g12, g22, g03, g13, g23, g33) = entry
    gram = [
        [g00, g01, g02, g03],
        [g01, g11, g12, g13],
        [g02, g12, g22, g23],
        [g03, g13, g23, g33],
    ]
    grow = 1.0 / SCALE
    image = [
        [SHIFTS[j] * gram[j][b] + grow * gram[j + 1][b] for b in range(ITERS + 1)]
        for j in range(ITERS)
    ]
    normal = [
        [SHIFTS[b] * image[a][b] + grow * image[a][b + 1] for b in range(ITERS)]
        for a in range(ITERS)
    ]
    target = [image[a][0] for a in range(ITERS)]
    for col in range(ITERS):
        for row in range(col + 1, ITERS):
            factor = normal[row][col] / normal[col][col]
            normal[row] = [normal[row][b] - factor * normal[col][b] for b in range(ITERS)]
            target[row] = target[row] - factor * target[col]
    coeffs = [None] * ITERS
    for row in range(ITERS - 1, -1, -1):
        acc = target[row]
        for b in range(row + 1, ITERS):
            acc = acc - normal[row][b] * coeffs[b]
        coeffs[row] = acc / normal[row][row]
    wide = [jnp.broadcast_to(c, (8, TILE)) for c in coeffs]

    def mix(ref, others):
        def rows(i, carry):
            at = pl.ds(pl.multiple_of(i * 8, 8), 8)
            ref[at, :] = (
                wide[0] * ref[at, :] + wide[1] * others[0][at, :] + wide[2] * others[1][at, :]
            )
            return carry

        return rows

    wait_all(get_s)
    lax.fori_loop(0, TILES // 8, mix(s0, (s1, s2)), 0, unroll=2)
    puts = [copies.start(s0, out_s)]
    for c, gets in enumerate(get_u):
        wait_all(gets)
        lax.fori_loop(c * PART // 8, (c + 1) * PART // 8, mix(u0, (u1, u2)), 0, unroll=8)
        at = pl.ds(c * PART, PART)
        puts.append(copies.start(u0.at[at], out_u.at[at]))
    wait_all(puts)


def finish(parts, fields, faces):
    scratch = [pltpu.VMEM(parts.shape, f32)] + [field()] * 3 + [on_faces()] * 3
    return call(finish_body, "finish", (parts, *fields, *faces), (FIELD, ON_FACES), scratch, 21)


def exchanged(sides):
    halos = []
    for axis, pair in zip(AXES, [sides[n : n + 2] for n in range(0, len(sides), 2)]):
        size = lax.axis_size(axis)
        even = [(i, i ^ 1) for i in range(size)]
        odd = [(i, i + 1) for i in range(1, size - 1, 2)]
        odd += [(b, a) for a, b in odd]
        halos += [lax.ppermute(pair[0], axis, even), lax.ppermute(pair[1], axis, odd)]
    return halos


def local(
    rhs_cells, heat_diag, rhs_faces, emissive, view_factors, tile_slots, read_lists, face_cells
):
    slab = ("gy", "gz")
    group = lax.axis_size(slab)
    group_z = lax.axis_size("gz")
    devices = lax.axis_size(AXES)
    slots = tile_slots.T
    reads = read_lists[0].T
    flat = (ROWS, CZ)
    fields, faces = [rhs_cells.reshape(flat)], [rhs_faces]
    heat = heat_diag.reshape(flat)
    for j in range(ITERS):
        u, s = fields[j], faces[j]
        if j == 0:
            base, under, sent, *sides = first(group, group_z, u, s, face_cells, heat)
            halos = exchanged(sides)
        all_faces = lax.all_to_all(sent, slab, 0, 0, tiled=True).reshape(-1, TILE)
        given = (slots, reads, u, base, all_faces, view_factors, emissive, under, s)
        if j + 1 < ITERS:
            u, s, sent, base, under, *sides = middle(
                j, group, group_z, *given, face_cells, heat, halos
            )
            halos = exchanged(sides)
            fields.append(u)
            faces.append(s)
        else:
            dots = last(devices, group_z, *given, *fields[:j], *faces[:j], halos)
    sums = lax.all_to_all(dots[:, None, :], AXES, 0, 0, tiled=True)
    sol_cells, sol_faces = finish(sums.reshape(devices, CZ), fields, faces)
    return (sol_cells.reshape(CX, CY, CZ), sol_faces)


def solution(mesh):
    placed = (
        P("gx", "gy", "gz"),
        P("gx", "gy", "gz"),
        P(("gx", "gy", "gz"), None),
        P(("gx", "gy", "gz"), None),
        P(("gx", "gy", "gz"), None, None, None),
        P(("gx", "gy", "gz"), None),
        P(("gx", "gy", "gz"), None, None),
        P(("gx", "gy", "gz"), None),
    )
    return jax.shard_map(
        local,
        mesh=mesh,
        in_specs=placed,
        out_specs=(P("gx", "gy", "gz"), P(("gx", "gy", "gz"), None)),
        check_vma=False,
    )
```
